128 devices in a mesh: context: 8 (over z, core), tensor: 16 (over x, y).
Axes of the slice: x: 4, y: 4, z: 4, core: 2. Of those that a mesh axis runs over, the one named last changes fastest.
Arguments:
- features: bfloat16 [4096, 3, 8192], P('context', None, 'tensor'), may hold values from -6 to 6
- se_filter: float32 [7, 3, 8192], P(None, None, 'tensor'), may hold values from -1.6 to 1.6
- mr_filter: bfloat16 [128, 512], P(None, 'tensor'), may hold values from -0.61 to 0.61
- stream: bfloat16 [4096, 8192], P('context', 'tensor'), may hold values from -20 to 20
- w_out: bfloat16 [8192, 8192], P('tensor'), may hold values from -0.09375 to 0.09375
- norm_gain: float32 [8192], replicated, may hold values from 0.1 to 1.9
- w_qkv: bfloat16 [8192, 3, 4096], P(None, None, 'tensor'), as said below
Outputs:
- stream_out: bfloat16 [4096, 8192], P('context', 'tensor')
- context_out: bfloat16 [4096, 4096], P('context', 'tensor')
The draws below stay inside these ranges and needn't reach their ends.
Inputs may be any that keep to these rules, and one draw needn't show every extreme that they name: `w_qkv`: projection weights.
All inputs are finite; a program needn't handle non-finite values.
Results may differ from the reference program's by a relative error of at most 0.019.
Values may be sent and summed in bfloat16 or wider, within the bound.
No kernel may reach another device: no remote copies, remote signals or barrier semaphores. Data moves between devices by JAX's collectives and lax.ppermute only.
A program may use at most 192 MiB of HBM per device.

```python
import math
import jax
import jax.numpy as jnp
from jax import lax

D = 8192
HEADS = 32
HD = 128
GROUP = 16
SE_K = 7
MR_K = 128
SEQ = 4096


def draw_mr_filter(key, part):
    groups_all = D // GROUP
    k_rate, k_tap = jax.random.split(jax.random.fold_in(key, 11), 2)
    rates = jnp.exp(jax.random.uniform(k_rate, (groups_all,), jnp.float32, math.log(1.0 / 400.0), math.log(1.0 / 25.0)))
    taps_raw = jax.random.truncated_normal(k_tap, -4.0, 4.0, (MR_K, groups_all), jnp.float32)
    lag_axis = jnp.arange(MR_K, dtype=jnp.float32)
    filtered = 0.15 * taps_raw * jnp.exp(-lag_axis[:, None] * rates[None, :])
    return filtered.astype(jnp.bfloat16)


def draw_stream(key, part):
    k_row, k_val = jax.random.split(jax.random.fold_in(key, 23), 2)
    column_pos = jnp.arange(D, dtype=jnp.float32) / D
    row_level = jax.random.uniform(k_row, (SEQ, 1), jnp.float32)
    values = jax.random.truncated_normal(k_val, -4.0, 4.0, (SEQ, D), jnp.float32)
    scaled = values * jnp.power(10.0, column_pos[None, :] + row_level - 1.3)
    return scaled.astype(jnp.bfloat16)


def draw_w_qkv(key, part):
    k_base = jax.random.fold_in(jax.random.fold_in(key, 37), 0)
    multiplier = jnp.array([1.6, 1.6, 1.0], jnp.float32)[None, :, None] / math.sqrt(D)
    base = jax.random.truncated_normal(k_base, -4.0, 4.0, (D, 3, HEADS * HD), jnp.float32) * multiplier
    return base.astype(jnp.bfloat16)


def strengthened(values, own_key, source, target, parts, factor):
    owner, partner = [(jnp.arange(values.shape[dim]) // (values.shape[dim] // parts)).reshape([-1 if axis == dim else 1 for axis in range(values.ndim)]) for dim in (source, target)]
    chosen = jax.random.permutation(own_key, parts)[partner]
    strong = (owner == chosen) | (owner == (partner + parts // 2) % parts)
    return jnp.where(strong, factor * values, values)


def shard_levels(own_key, shape, pieces, low, top_value):
    level = 1.0
    for dim, shards_of in pieces:
        draws = jax.random.uniform(jax.random.fold_in(jax.random.fold_in(own_key, 6), dim), (shards_of,), jnp.float32, low / len(pieces), top_value / len(pieces))
        level = level * jnp.repeat(jnp.exp(draws), shape[dim] // shards_of).reshape((-1,) + (1,) * (len(shape) - 1 - dim))
    return level


def gaussian(key, shape, scale, limit, cuts=(), kind=jnp.bfloat16):
    values = scale * jax.random.normal(key, shape, jnp.float32)
    if cuts:
        values = values * shard_levels(key, shape, cuts, -0.22, 0.18)
    return jnp.clip(values, -limit, limit).astype(kind)


def bell_draw_with(stream_key, dims, deviation, bound, cuts, heavy, kind=jnp.bfloat16):
    values = deviation * jax.random.normal(stream_key, dims, jnp.float32)
    if cuts:
        values = values * shard_levels(stream_key, dims, cuts, -0.22, 0.18)
    return jnp.clip(strengthened(values, jax.random.fold_in(stream_key, 3), *heavy), -bound, bound).astype(kind)


def setup_inputs(seed: int = 0) -> dict:
    key_list = jax.random.split(jax.random.key(seed), 8)
    return {
        "features": gaussian(key_list[0], (SEQ, 3, D), 1.0, 6.0, ((0, 8), (2, 16))),
        "se_filter": gaussian(key_list[1], (SE_K, 3, D), 0.4, 1.6, ((2, 16),), jnp.float32),
        "mr_filter": draw_mr_filter(jax.random.fold_in(key_list[7], 71), 0),
        "stream": draw_stream(jax.random.fold_in(key_list[7], 71), 0),
        "w_out": bell_draw_with(key_list[4], (D, D), D ** -0.5, 0.09375, ((0, 16),), (0, 1, 16, 2.0)),
        "norm_gain": jnp.clip(1.0 + 0.18 * jax.random.normal(key_list[5], (D,), jnp.float32), 0.1, 1.9),
        "w_qkv": draw_w_qkv(jax.random.fold_in(key_list[7], 71), 0),
    }


def reference(features, se_filter, mr_filter, stream, w_out, norm_gain, w_qkv):
    feature_f32 = features.astype(jnp.float32)
    padded = jnp.pad(feature_f32, ((SE_K - 1, 0), (0, 0), (0, 0)))
    short_out = se_filter[0][None] * padded[SE_K - 1:SE_K - 1 + SEQ]
    for offset_lag in range(1, SE_K):
        short_out = short_out + se_filter[offset_lag][None] * padded[SE_K - 1 - offset_lag:SE_K - 1 - offset_lag + SEQ]
    kv_prod = (short_out[:, 1, :] * short_out[:, 2, :]).astype(jnp.bfloat16)
    group_taps = jnp.repeat(mr_filter.astype(jnp.float32), GROUP, axis=1)
    kv_padded = jnp.pad(kv_prod.astype(jnp.float32), ((MR_K - 1, 0), (0, 0)))

    def lag_step(offset_lag, running):
        window = lax.dynamic_slice_in_dim(kv_padded, MR_K - 1 - offset_lag, SEQ, 0)
        tap_row = lax.dynamic_slice_in_dim(group_taps, offset_lag, 1, 0)
        return running + tap_row * window
    medium = lax.fori_loop(0, MR_K, lag_step, jnp.zeros((SEQ, D), jnp.float32))
    gated = (short_out[:, 0, :] * medium).astype(jnp.bfloat16)
    mixed_rows = stream.astype(jnp.float32) + jnp.dot(gated, w_out, preferred_element_type=jnp.float32)
    stream_out = mixed_rows.astype(jnp.bfloat16)
    mean_square = lax.optimization_barrier(jnp.mean(mixed_rows * mixed_rows, axis=1, keepdims=True))
    normed = (mixed_rows * lax.rsqrt(mean_square + 1e-05) * norm_gain[None, :]).astype(jnp.bfloat16)
    qkv_proj = jnp.dot(normed, w_qkv.reshape(D, 3 * HEADS * HD), preferred_element_type=jnp.float32)
    qkv_proj = qkv_proj.astype(jnp.bfloat16).reshape(SEQ, 3, HEADS, HD)
    query_heads = jnp.transpose(qkv_proj[:, 0], (1, 0, 2))
    key_heads = jnp.transpose(qkv_proj[:, 1], (1, 0, 2))
    value_heads = jnp.transpose(qkv_proj[:, 2], (1, 0, 2))
    position = jnp.arange(SEQ)
    causal = position[None, :] <= position[:, None]
    scale_factor = 1.0 / math.sqrt(HD)

    def one_head(triple):
        query, keys_all, values = triple
        scores = jnp.dot(query, keys_all.T, preferred_element_type=jnp.float32) * scale_factor
        scores = jnp.where(causal, scores, -jnp.inf)
        row_max = lax.optimization_barrier(jnp.max(scores, axis=1, keepdims=True))
        expo = jnp.exp(scores - row_max)
        row_total = lax.optimization_barrier(jnp.sum(expo, axis=1, keepdims=True))
        weights = expo.astype(jnp.bfloat16)
        return jnp.dot(weights, values, preferred_element_type=jnp.float32) / row_total
    attended = lax.map(one_head, (query_heads, key_heads, value_heads))
    context_out = jnp.transpose(attended, (1, 0, 2)).reshape(SEQ, HEADS * HD).astype(jnp.bfloat16)
    return (stream_out, context_out)
```

```python
import jax
import jax.numpy as jnp
from jax import lax
from jax.experimental import pallas as pl
from jax.experimental.pallas import tpu as pltpu
from jax.sharding import PartitionSpec as P

HD = 128
SIDE = 4
GRID = 16
HALO = 144
VMEM_LIMIT = 56 * 1024 * 1024
BF = jnp.bfloat16
F32 = jnp.float32


def params(**kw):
    return pltpu.CompilerParams(vmem_limit_bytes=VMEM_LIMIT, **kw)


def hop(value, dx, dy):
    pairs = []
    for x in range(SIDE):
        for y in range(SIDE):
            pairs.append((x * SIDE + y, ((x + dx) % SIDE) * SIDE + (y + dy) % SIDE))
    return lax.ppermute(value, "tensor", pairs)


def hop_z(value, steps):
    pairs = [(z * 2 + core, to * 2 + core) for z, to in steps for core in range(2)]
    return lax.ppermute(value, "context", pairs)


def swap_core(value):
    return lax.ppermute(value, "context", [(c, c ^ 1) for c in range(2 * SIDE)])


def toeplitz_body(taps, out):
    for g in range(taps.shape[0]):
        row = jnp.broadcast_to(taps[g : g + 1, :], (128, 256))
        out[g] = pltpu.roll(row, 1, 1, stride=1, stride_axis=0).astype(BF)


def toeplitz(mr_filter):
    groups = mr_filter.shape[1]
    taps = jnp.pad(mr_filter[::-1].T.astype(F32), ((0, 0), (0, 128)))
    return pl.pallas_call(
        toeplitz_body,
        grid=(groups // 8,),
        in_specs=[pl.BlockSpec((8, 256), lambda i: (i, 0))],
        out_specs=pl.BlockSpec((8, 128, 256), lambda i: (i, 0, 0)),
        out_shape=jax.ShapeDtypeStruct((groups, 128, 256), BF),
        compiler_params=params(),
        name="toeplitz",
    )(taps)


def filters_body(feats, halo, taps, toep, out, x0, x1, x2, kvs):
    rows = feats.shape[1]
    x0[0:16] = halo[0:16].astype(F32)
    x0[16:] = feats[0].astype(F32)
    x1[0:HALO] = halo[16 : 16 + HALO].astype(F32)
    x1[HALO:] = feats[1].astype(F32)
    x2[0:HALO] = halo[16 + HALO : 16 + 2 * HALO].astype(F32)
    x2[HALO:] = feats[2].astype(F32)
    width = taps.shape[1]

    def short(ref, j, start):
        total = taps[j, 0:1, :] * ref[start : start + 128]
        for s in range(1, width):
            total = total + taps[j, s : s + 1, :] * ref[start - s : start - s + 128]
        return total

    for b in range(rows // 128 + 1):
        start = HALO - 128 + b * 128
        kvs[b * 128 : (b + 1) * 128] = (short(x1, 1, start) * short(x2, 2, start)).astype(BF)
    lane_group = lax.broadcasted_iota(jnp.int32, (128, 128), 1) // 16
    lhs = toep[...].reshape(8 * 128, 256)
    for b in range(rows // 128):
        full = jnp.dot(lhs, kvs[b * 128 : b * 128 + 256], preferred_element_type=F32)
        medium = full[0:128]
        for g in range(1, 8):
            medium = jnp.where(lane_group == g, full[g * 128 : (g + 1) * 128], medium)
        out[b * 128 : (b + 1) * 128] = (short(x0, 0, 16 + b * 128) * medium).astype(BF)


def filters(feats, halo, taps, toep):
    rows, chans = feats.shape[1:]
    return pl.pallas_call(
        filters_body,
        grid=(chans // 128,),
        in_specs=[
            pl.BlockSpec((3, rows, 128), lambda i: (0, 0, i)),
            pl.BlockSpec((halo.shape[0], 128), lambda i: (0, i)),
            pl.BlockSpec((3, taps.shape[1], 128), lambda i: (0, 0, i)),
            pl.BlockSpec((8, 128, 256), lambda i: (i, 0, 0)),
        ],
        out_specs=pl.BlockSpec((rows, 128), lambda i: (0, i)),
        out_shape=jax.ShapeDtypeStruct((rows, chans), BF),
        scratch_shapes=[
            pltpu.VMEM((rows + 16, 128), F32),
            pltpu.VMEM((rows + HALO, 128), F32),
            pltpu.VMEM((rows + HALO, 128), F32),
            pltpu.VMEM((rows + 128, 128), BF),
        ],
        compiler_params=params(),
        name="filters",
    )(feats, halo, taps, toep)


PIECES = (("p", 4), ("m", 4), ("1a", 2), ("3b", 2), ("0", 4))


def piece_of(far, near):
    if far == 0:
        return "0", near
    if far == 2:
        return ("p", near) if near < 2 else ("m", near - 2)
    if far == 1:
        return ("1a", near) if near < 2 else ("p", near)
    return ("m", near + 2) if near < 2 else ("3b", near - 2)


def project_body(rank, gated, w_hbm, *refs):
    count = len(PIECES)
    outs, (wbuf, obuf, wsem, osem) = refs[: 2 * count], refs[2 * count :]
    names = [name for name, _ in PIECES]
    a_out = dict(zip(names, outs[:count], strict=True))
    b_out = dict(zip(names, outs[count:], strict=True))
    x, y = rank[0] // SIDE, rank[0] % SIDE
    cols = gated.shape[1]
    half = gated.shape[0] // 2
    order = [(dx, dy) for dx in range(SIDE) for dy in range(SIDE)]
    fetches, stores = [], []
    for i, (dx, dy) in enumerate(order):
        index = lax.rem(x + dx, SIDE) * SIDE + lax.rem(y + dy, SIDE)
        copy = pltpu.make_async_copy(
            w_hbm.at[:, pl.ds(pl.multiple_of(index * cols, cols), cols)], wbuf.at[i], wsem.at[i]
        )
        copy.start()
        fetches.append(copy)
    for i, (dx, dy) in enumerate(order):
        fetches[i].wait()
        obuf[i] = jnp.dot(gated[...], wbuf[i], preferred_element_type=F32).astype(BF)
        name, place = piece_of(dx, dy)
        low = pltpu.make_async_copy(obuf.at[i, 0:half], a_out[name].at[place], osem.at[2 * i])
        name, place = piece_of(dy, dx)
        high = pltpu.make_async_copy(
            obuf.at[i, half : 2 * half], b_out[name].at[place], osem.at[2 * i + 1]
        )
        low.start()
        high.start()
        stores += [low, high]
    for copy in stores:
        copy.wait()


def project(rank, gated, w_out):
    rows, cols = gated.shape
    shapes = [jax.ShapeDtypeStruct((n, rows // 2, cols), BF) for _, n in PIECES] * 2
    outs = pl.pallas_call(
        project_body,
        in_specs=[
            pl.BlockSpec(memory_space=pltpu.SMEM),
            pl.BlockSpec(memory_space=pltpu.VMEM),
            pl.BlockSpec(memory_space=pl.ANY),
        ],
        out_specs=[pl.BlockSpec(memory_space=pl.ANY)] * len(shapes),
        out_shape=shapes,
        scratch_shapes=[
            pltpu.VMEM((GRID, rows, cols), BF),
            pltpu.VMEM((GRID, rows, cols), BF),
            pltpu.SemaphoreType.DMA((GRID,)),
            pltpu.SemaphoreType.DMA((2 * GRID,)),
        ],
        compiler_params=params(),
        cost_estimate=pl.CostEstimate(
            flops=2 * rows * w_out.size, transcendentals=0, bytes_accessed=4 * w_out.size
        ),
        name="project",
    )(rank, gated, w_out)
    names = [name for name, _ in PIECES]
    count = len(names)
    return dict(zip(names, outs[:count], strict=True)), dict(zip(names, outs[count:], strict=True))


def plus(*terms):
    total = terms[0].astype(F32)
    for term in terms[1:]:
        total = total + term.astype(F32)
    return total


def reduce_half(p, first, second):
    rp = first(p["p"], 1)
    rm = first(p["m"], -1)
    r1a = first(plus(p["1a"], rp[0:2]).astype(BF), 1)
    r3b = first(plus(p["3b"], rm[0:2]).astype(BF), -1)
    low = plus(p["0"][0:2], rm[2:4], r1a)
    high = plus(p["0"][2:4], rp[2:4], r3b)
    mine, one, two, three = low[0], low[1], high[0], high[1]
    h = mine.shape[0] // 2
    sp = second(jnp.concatenate([two[:h], one[h:]], axis=0).astype(BF), 1)
    sm = second(jnp.concatenate([two[h:], three[:h]], axis=0).astype(BF), -1)
    s1a = second(plus(one[:h], sp[:h]).astype(BF), 1)
    s3b = second(plus(three[h:], sm[:h]).astype(BF), -1)
    return plus(mine, jnp.concatenate([s1a, s3b], axis=0), jnp.concatenate([sm[h:], sp[h:]], axis=0))


def gather_half(own, first, second):
    h = own.shape[0] // 2
    back = first(own, 1)
    ahead = first(own, -1)
    far = jnp.concatenate([first(back[:h], 1), first(ahead[h:], -1)], axis=0)
    line = (0, 3, 1, 2)
    block = jnp.stack([own, back, ahead, far])
    from_back = second(block, 1)
    from_ahead = second(block, -1)
    near = [(block, [(d, 0) for d in line])]
    mid = [(from_back, [(d, 3) for d in line]), (from_ahead, [(d, 1) for d in line])]
    last = [
        (second(from_back[0:2], 1), [(d, 2) for d in line[0:2]]),
        (second(from_ahead[2:4], -1), [(d, 2) for d in line[2:4]]),
    ]
    return near, mid, last


def qkv_body(spec, has_acc, last, rank, w_hbm, gain, *refs):
    refs = list(refs)
    acc_in = refs.pop(0) if has_acc else None
    count = len(spec)
    pieces, refs = refs[:count], refs[count:]
    if last:
        q_out, kv_out, acc, wbuf, wsem = refs
    else:
        acc, wbuf, wsem = refs
    x, y = rank[0] // SIDE, rank[0] % SIDE
    slots = []
    for places, _ in spec:
        for place in places:
            if place not in slots:
                slots.append(place)
    depth, part = wbuf.shape[2:]
    ahead = wbuf.shape[0]

    def index(i):
        dx, dy = slots[i]
        return lax.rem(x + dx, SIDE) * SIDE + lax.rem(y + dy, SIDE)

    def fetch(i):
        copy = pltpu.make_async_copy(
            w_hbm.at[:, pl.ds(pl.multiple_of(index(i) * depth, depth), depth), :],
            wbuf.at[i % ahead],
            wsem.at[i % ahead],
        )
        copy.start()
        return copy

    copies = [fetch(i) for i in range(min(ahead, len(slots)))]
    if has_acc:
        acc[...] = acc_in[...]
    else:
        acc[...] = jnp.zeros_like(acc)
    for i, slot in enumerate(slots):
        copies[i].wait()
        gains = gain[pl.ds(index(i), 1), :]
        for (places, row), ref in zip(spec, pieces, strict=True):
            for k, place in enumerate(places):
                if place != slot:
                    continue
                value = ref[k].astype(F32)
                rows = pl.ds(row, value.shape[0])
                square = value * value
                for c in range(0, depth, 128):
                    acc[rows, 3 * part :] += square[:, c : c + 128]
                value = (value * gains).astype(BF)
                for j in range(3):
                    acc[rows, j * part : (j + 1) * part] += jnp.dot(
                        value, wbuf[i % ahead, j], preferred_element_type=F32
                    )
        if i + ahead < len(slots):
            copies.append(fetch(i + ahead))
    if last:
        mean = jnp.sum(acc[:, 3 * part :], axis=1, keepdims=True) / (depth * GRID)
        scale = lax.rsqrt(mean + 1e-05)
        q_out[...] = (acc[:, :part] * scale).astype(BF)
        kv_out[...] = (acc[:, part : 3 * part] * scale).astype(BF)


def qkv_part(rank, w, gain, pieces, acc, last):
    spec = [(places, row) for _, places, row in pieces]
    part = w.shape[2]
    half, depth = pieces[0][0].shape[1:]
    rows = 2 * half
    vmem = pl.BlockSpec(memory_space=pltpu.VMEM)
    args = [rank, w, gain]
    specs = [pl.BlockSpec(memory_space=pltpu.SMEM), pl.BlockSpec(memory_space=pl.ANY), vmem]
    if acc is not None:
        args.append(acc)
        specs.append(vmem)
    for piece in pieces:
        args.append(piece[0])
        specs.append(vmem)
    scratch = [pltpu.VMEM((4, 3, depth, part), BF), pltpu.SemaphoreType.DMA((4,))]
    acc_shape = (rows, 3 * part + 128)
    if last:
        out_shape = [
            jax.ShapeDtypeStruct((rows, part), BF),
            jax.ShapeDtypeStruct((rows, 2 * part), BF),
        ]
        out_specs = [vmem, vmem]
        scratch = [pltpu.VMEM(acc_shape, F32)] + scratch
    else:
        out_shape = jax.ShapeDtypeStruct(acc_shape, F32)
        out_specs = vmem

    def body(*refs):
        qkv_body(spec, acc is not None, last, *refs)

    blocks = sum(len(places) for places, _ in spec)
    return pl.pallas_call(
        body,
        in_specs=specs,
        out_specs=out_specs,
        out_shape=out_shape,
        scratch_shapes=scratch,
        compiler_params=params(),
        cost_estimate=pl.CostEstimate(
            flops=blocks * 2 * half * depth * 3 * part,
            transcendentals=0,
            bytes_accessed=blocks * 6 * depth * part,
        ),
        name="qkv",
    )(*args)


def attend_body(count, flags, q, *refs):
    kvs, refs = refs[:count], refs[count:]
    out, m_s, l_s, acc_s = refs
    heads = q.shape[1] // HD
    rows = q.shape[0]
    tile = 256
    factor = HD ** (-0.5)

    def step(ref, h, r, keys, first, masked):
        part = heads * HD
        query = q[r : r + tile, h * HD : (h + 1) * HD]
        key = ref[0:keys, h * HD : (h + 1) * HD]
        value = ref[0:keys, part + h * HD : part + (h + 1) * HD]
        s = lax.dot_general(
            query, key, (((1,), (1,)), ((), ())), preferred_element_type=F32
        ) * factor
        if masked:
            qpos = r + lax.broadcasted_iota(jnp.int32, s.shape, 0)
            kpos = lax.broadcasted_iota(jnp.int32, s.shape, 1)
            s = jnp.where(kpos <= qpos, s, -1e30)
        top = jnp.max(s, axis=1, keepdims=True)
        if first:
            new = top
        else:
            old = m_s[h, r : r + tile]
            new = jnp.maximum(old, top)
        e = jnp.exp(s - new)
        total = jnp.sum(e, axis=1, keepdims=True)
        mixed = jnp.dot(e.astype(BF), value, preferred_element_type=F32)
        if first:
            l_s[h, r : r + tile] = total
            acc_s[h, r : r + tile] = mixed
        else:
            fade = jnp.exp(old - new)
            l_s[h, r : r + tile] = l_s[h, r : r + tile] * fade + total
            acc_s[h, r : r + tile] = acc_s[h, r : r + tile] * fade + mixed
        m_s[h, r : r + tile] = new

    for h in range(heads):
        for r in range(0, rows, tile):
            step(kvs[0], h, r, r + tile, True, True)
    for i in range(1, count):

        @pl.when(flags[i] == 1)
        def _(i=i):
            for h in range(heads):
                for r in range(0, rows, tile):
                    step(kvs[i], h, r, kvs[i].shape[0], False, False)

    for h in range(heads):
        out[:, h * HD : (h + 1) * HD] = (acc_s[h] / l_s[h]).astype(BF)


def attend(flags, q, kvs):
    rows, width = q.shape
    heads = width // HD
    count = len(kvs)
    vmem = pl.BlockSpec(memory_space=pltpu.VMEM)

    def body(*refs):
        attend_body(count, *refs)

    return pl.pallas_call(
        body,
        in_specs=[pl.BlockSpec(memory_space=pltpu.SMEM)] + [vmem] * (count + 1),
        out_specs=vmem,
        out_shape=jax.ShapeDtypeStruct((rows, width), BF),
        scratch_shapes=[
            pltpu.VMEM((heads, rows, 1), F32),
            pltpu.VMEM((heads, rows, 1), F32),
            pltpu.VMEM((heads, rows, HD), F32),
        ],
        compiler_params=params(),
        name="attend",
    )(flags, q, *kvs)


def on_device(features, se_filter, mr_filter, stream, w_out, norm_gain, w_qkv):
    rows, _, cols = features.shape
    feats = jnp.transpose(features, (1, 0, 2))
    taps = jnp.transpose(se_filter, (1, 0, 2))
    weights = jnp.transpose(w_qkv, (1, 0, 2))
    tensor_rank = lax.axis_index("tensor")
    context_rank = lax.axis_index("context")
    rank = tensor_rank.astype(jnp.int32).reshape(1)

    edge = jnp.concatenate(
        [feats[0, rows - 16 :], feats[1, rows - HALO :], feats[2, rows - HALO :]], axis=0
    )
    halo = lax.ppermute(edge, "context", [(c, c + 1) for c in range(2 * SIDE - 1)])
    gated = filters(feats, halo, taps, toeplitz(mr_filter))

    a, b = project(rank, gated, w_out)
    along_x = lambda v, d: hop(v, d, 0)
    along_y = lambda v, d: hop(v, 0, d)
    half = rows // 2
    own_a = (reduce_half(a, along_x, along_y) + stream[:half].astype(F32)).astype(BF)
    own_b = (reduce_half(b, along_y, along_x) + stream[half:].astype(F32)).astype(BF)
    stream_out = jnp.concatenate([own_a, own_b], axis=0)
    gain = norm_gain.reshape(GRID, cols)
    parts_a = gather_half(own_a, along_y, along_x)
    parts_b = gather_half(own_b, along_x, along_y)
    acc = None
    for i in range(3):
        pieces = [(v, [(dx, dy) for dy, dx in places], 0) for v, places in parts_a[i]]
        pieces += [(v, places, half) for v, places in parts_b[i]]
        acc = qkv_part(rank, weights, gain, pieces, acc, i == 2)
    query, kv = acc

    h = rows // 2
    back = hop_z(kv, ((0, 1), (1, 2), (2, 3)))
    ahead = hop_z(kv, ((0, 3), (1, 0)))
    far_one = hop_z(back[:h], ((1, 2), (2, 3)))
    far_two = hop_z(ahead[h:], ((3, 2), (0, 3)))
    z, core = context_rank // 2, context_rank % 2
    same = [(back, 3), (ahead, 1), (far_one, 2), (far_two, 2)]
    kvs = [kv, swap_core(kv)]
    flags = [jnp.int32(1), (core == 1).astype(jnp.int32)]
    for v, d in same:
        kvs += [v, swap_core(v)]
        flags += [((z + d) % SIDE < z).astype(jnp.int32)] * 2
    context_out = attend(jnp.stack(flags), query, kvs)
    return stream_out, context_out


def solution(mesh):
    placed = (
        P("context", None, "tensor"),
        P(None, None, "tensor"),
        P(None, "tensor"),
        P("context", "tensor"),
        P("tensor", None),
        P(),
        P(None, None, "tensor"),
    )
    return jax.shard_map(
        on_device,
        mesh=mesh,
        in_specs=placed,
        out_specs=(P("context", "tensor"), P("context", "tensor")),
        check_vma=False,
    )
```

```python
import math

import jax
import jax.numpy as jnp
from jax import lax
from jax.experimental import pallas as pl
from jax.experimental.pallas import tpu as pltpu
from jax.sharding import PartitionSpec as P

HD = 128
SIDE = 4
GRID = 16
HALO = 144
BF = jnp.bfloat16
F32 = jnp.float32


def params(mib):
    return pltpu.CompilerParams(vmem_limit_bytes=mib * 1024 * 1024)


def hop(value, dx, dy):
    pairs = []
    for x in range(SIDE):
        for y in range(SIDE):
            pairs.append((x * SIDE + y, ((x + dx) % SIDE) * SIDE + (y + dy) % SIDE))
    return lax.ppermute(value, "tensor", pairs)


def hop_z(value, steps):
    pairs = [(z * 2 + core, to * 2 + core) for z, to in steps for core in range(2)]
    return lax.ppermute(value, "context", pairs)


def swap_core(value):
    return lax.ppermute(value, "context", [(c, c ^ 1) for c in range(2 * SIDE)])


def toeplitz_body(taps, out):
    for g in range(taps.shape[0]):
        row = jnp.broadcast_to(taps[g : g + 1, :], (128, 256))
        out[g] = pltpu.roll(row, 1, 1, stride=1, stride_axis=0).astype(BF)


def toeplitz(mr_filter):
    groups = mr_filter.shape[1]
    taps = jnp.pad(mr_filter[::-1].T.astype(F32), ((0, 0), (0, 128)))
    return pl.pallas_call(
        toeplitz_body,
        grid=(groups // 8,),
        in_specs=[pl.BlockSpec((8, 256), lambda i: (i, 0))],
        out_specs=pl.BlockSpec((8, 128, 256), lambda i: (i, 0, 0)),
        out_shape=jax.ShapeDtypeStruct((groups, 128, 256), BF),
        compiler_params=params(16),
        name="toeplitz",
    )(taps)


def filters_body(feats, halo, taps, toep, out, x0, x1, x2, kvs):
    rows = feats.shape[1]
    x0[0:16] = halo[0:16].astype(F32)
    x0[16:] = feats[0].astype(F32)
    x1[0:HALO] = halo[16 : 16 + HALO].astype(F32)
    x1[HALO:] = feats[1].astype(F32)
    x2[0:HALO] = halo[16 + HALO : 16 + 2 * HALO].astype(F32)
    x2[HALO:] = feats[2].astype(F32)
    width = taps.shape[1]

    def short(ref, j, start):
        total = taps[j, 0:1, :] * ref[start : start + 128]
        for s in range(1, width):
            total = total + taps[j, s : s + 1, :] * ref[start - s : start - s + 128]
        return total

    for b in range(rows // 128 + 1):
        start = HALO - 128 + b * 128
        kvs[b * 128 : (b + 1) * 128] = (short(x1, 1, start) * short(x2, 2, start)).astype(BF)
    lane_group = lax.broadcasted_iota(jnp.int32, (128, 128), 1) // 16
    lhs = toep[...].reshape(8 * 128, 256)
    for b in range(rows // 128):
        full = jnp.dot(lhs, kvs[b * 128 : b * 128 + 256], preferred_element_type=F32)
        medium = full[0:128]
        for g in range(1, 8):
            medium = jnp.where(lane_group == g, full[g * 128 : (g + 1) * 128], medium)
        out[b * 128 : (b + 1) * 128] = (short(x0, 0, 16 + b * 128) * medium).astype(BF)


def filters(feats, halo, taps, toep):
    rows, chans = feats.shape[1:]
    return pl.pallas_call(
        filters_body,
        grid=(chans // 128,),
        in_specs=[
            pl.BlockSpec((3, rows, 128), lambda i: (0, 0, i)),
            pl.BlockSpec((halo.shape[0], 128), lambda i: (0, i)),
            pl.BlockSpec((3, taps.shape[1], 128), lambda i: (0, 0, i)),
            pl.BlockSpec((8, 128, 256), lambda i: (i, 0, 0)),
        ],
        out_specs=pl.BlockSpec((rows, 128), lambda i: (0, i)),
        out_shape=jax.ShapeDtypeStruct((rows, chans), BF),
        scratch_shapes=[
            pltpu.VMEM((rows + 16, 128), F32),
            pltpu.VMEM((rows + HALO, 128), F32),
            pltpu.VMEM((rows + HALO, 128), F32),
            pltpu.VMEM((rows + 128, 128), BF),
        ],
        compiler_params=params(16),
        name="filters",
    )(feats, halo, taps, toep)


PIECES = (("p", 4), ("m", 4), ("1a", 2), ("3b", 2), ("0", 4))


def piece_of(far, near):
    if far == 0:
        return "0", near
    if far == 2:
        return ("p", near) if near < 2 else ("m", near - 2)
    if far == 1:
        return ("1a", near) if near < 2 else ("p", near)
    return ("m", near + 2) if near < 2 else ("3b", near - 2)


def project_body(rank, gated, w, *refs):
    count = len(PIECES)
    names = [name for name, _ in PIECES]
    a_out = dict(zip(names, refs[:count], strict=True))
    b_out = dict(zip(names, refs[count:], strict=True))
    x, y = rank[0] // SIDE, rank[0] % SIDE
    cols = gated.shape[1]
    half = gated.shape[0] // 2
    for dx in range(SIDE):
        for dy in range(SIDE):
            index = lax.rem(x + dx, SIDE) * SIDE + lax.rem(y + dy, SIDE)
            block = jnp.dot(
                gated[...],
                w[:, pl.ds(pl.multiple_of(index * cols, cols), cols)],
                preferred_element_type=F32,
            ).astype(BF)
            name, place = piece_of(dx, dy)
            a_out[name][place] = block[:half]
            name, place = piece_of(dy, dx)
            b_out[name][place] = block[half:]


def project(rank, gated, w_out):
    rows, cols = gated.shape
    shapes = [jax.ShapeDtypeStruct((n, rows // 2, cols), BF) for _, n in PIECES] * 2
    vmem = pl.BlockSpec(memory_space=pltpu.VMEM)
    outs = pl.pallas_call(
        project_body,
        in_specs=[pl.BlockSpec(memory_space=pltpu.SMEM), vmem, vmem],
        out_specs=[vmem] * len(shapes),
        out_shape=shapes,
        compiler_params=params(24),
        cost_estimate=pl.CostEstimate(
            flops=2 * rows * w_out.size, transcendentals=0, bytes_accessed=4 * w_out.size
        ),
        name="project",
    )(rank, gated, w_out)
    names = [name for name, _ in PIECES]
    count = len(names)
    return dict(zip(names, outs[:count], strict=True)), dict(zip(names, outs[count:], strict=True))


def plus(*terms):
    total = terms[0].astype(F32)
    for term in terms[1:]:
        total = total + term.astype(F32)
    return total


def reduce_half(p, first, second):
    rp = first(p["p"], 1)
    rm = first(p["m"], -1)
    r1a = first(plus(p["1a"], rp[0:2]).astype(BF), 1)
    r3b = first(plus(p["3b"], rm[0:2]).astype(BF), -1)
    low = plus(p["0"][0:2], rm[2:4], r1a)
    high = plus(p["0"][2:4], rp[2:4], r3b)
    mine, one, two, three = low[0], low[1], high[0], high[1]
    h = mine.shape[0] // 2
    sp = second(jnp.concatenate([two[:h], one[h:]], axis=0).astype(BF), 1)
    sm = second(jnp.concatenate([two[h:], three[:h]], axis=0).astype(BF), -1)
    s1a = second(plus(one[:h], sp[:h]).astype(BF), 1)
    s3b = second(plus(three[h:], sm[:h]).astype(BF), -1)
    return plus(mine, jnp.concatenate([s1a, s3b], axis=0), jnp.concatenate([sm[h:], sp[h:]], axis=0))


LINE = (0, 3, 1, 2)


def gather_line(own, first, second):
    h = own.shape[0] // 2
    back = first(own, 1)
    ahead = first(own, -1)
    far = jnp.concatenate([first(back[:h], 1), first(ahead[h:], -1)], axis=0)
    block = jnp.stack([own, back, ahead, far])
    return block, second(block, 1), second(block, -1)


def gather_rest(back, ahead, acc, second):
    back, _ = lax.optimization_barrier((back, acc))
    ahead, _ = lax.optimization_barrier((ahead, acc))
    return second(back[0:2], 1), second(ahead[2:4], -1)


def qkv_body(spec, has_acc, last, rank, w_hbm, gain, *refs):
    refs = list(refs)
    acc_in = refs.pop(0) if has_acc else None
    count = len(spec)
    pieces, refs = refs[:count], refs[count:]
    if last:
        q_out, kv_out, acc, xbuf, wbuf, wsem = refs
    else:
        acc, xbuf, wbuf, wsem = refs
    x, y = rank[0] // SIDE, rank[0] % SIDE
    part = wbuf.shape[3]
    depth = gain.shape[1]

    def index(place):
        return lax.rem(x + place[0], SIDE) * SIDE + lax.rem(y + place[1], SIDE)

    def fetch(i):
        copies = []
        for k, place in enumerate(spec[i][0]):
            copy = pltpu.make_async_copy(
                w_hbm.at[:, pl.ds(pl.multiple_of(index(place) * depth, depth), depth), :],
                wbuf.at[i % 2, :, k * depth : (k + 1) * depth, :],
                wsem.at[i % 2, k],
            )
            copy.start()
            copies.append(copy)
        return copies

    fetched = [fetch(i) for i in range(2)]
    filled = set()
    for i, ((places, row), ref) in enumerate(zip(spec, pieces, strict=True)):
        total = None
        rows = pl.ds(row, ref.shape[1])
        for k, place in enumerate(places):
            value = ref[k].astype(F32)
            for c in range(0, depth, 128):
                square = value[:, c : c + 128] * value[:, c : c + 128]
                total = square if total is None else total + square
            gains = gain[pl.ds(index(place), 1), :]
            xbuf[:, k * depth : (k + 1) * depth] = (value * gains).astype(BF)
        for copy in fetched[i]:
            copy.wait()
        wide = len(places) * depth
        if row in filled:
            before = acc
        else:
            before = acc_in
        filled.add(row)
        for j in range(3):
            cols = slice(j * part, (j + 1) * part)
            term = jnp.dot(xbuf[:, :wide], wbuf[i % 2, j, :wide], preferred_element_type=F32)
            acc[rows, cols] = term if before is None else before[rows, cols] + term
        acc[rows, 3 * part :] = total if before is None else before[rows, 3 * part :] + total
        if i + 2 < count:
            fetched.append(fetch(i + 2))
    if last:
        mean = jnp.sum(acc[:, 3 * part :], axis=1, keepdims=True) / (depth * GRID)
        scale = lax.rsqrt(mean + 1e-05)
        kv_out[...] = (acc[:, part : 3 * part] * scale).astype(BF)
        q_out[...] = (acc[:, :part] * scale).astype(BF)


def qkv_part(rank, w, gain, pieces, acc, last):
    spec = [(places, row) for _, places, row in pieces]
    part = w.shape[2]
    half, depth = pieces[0][0].shape[1:]
    deep = max(len(places) for places, _ in spec) * depth
    rows = 2 * half
    vmem = pl.BlockSpec(memory_space=pltpu.VMEM)
    args = [rank, w, gain]
    specs = [pl.BlockSpec(memory_space=pltpu.SMEM), pl.BlockSpec(memory_space=pl.ANY), vmem]
    if acc is not None:
        args.append(acc)
        specs.append(vmem)
    for piece in pieces:
        args.append(piece[0])
        specs.append(vmem)
    scratch = [
        pltpu.VMEM((half, deep), BF),
        pltpu.VMEM((2, 3, deep, part), BF),
        pltpu.SemaphoreType.DMA((2, 4)),
    ]
    acc_shape = (rows, 3 * part + 128)
    if last:
        out_shape = [
            jax.ShapeDtypeStruct((rows, part), BF),
            jax.ShapeDtypeStruct((rows, 2 * part), BF),
        ]
        out_specs = [vmem, vmem]
        scratch = [pltpu.VMEM(acc_shape, F32)] + scratch
    else:
        out_shape = jax.ShapeDtypeStruct(acc_shape, F32)
        out_specs = vmem

    def body(*refs):
        qkv_body(spec, acc is not None, last, *refs)

    blocks = sum(len(places) for places, _ in spec)
    return pl.pallas_call(
        body,
        in_specs=specs,
        out_specs=out_specs,
        out_shape=out_shape,
        scratch_shapes=scratch,
        compiler_params=params(24),
        cost_estimate=pl.CostEstimate(
            flops=blocks * 2 * half * depth * 3 * part,
            transcendentals=0,
            bytes_accessed=blocks * 6 * depth * part,
        ),
        name="qkv",
    )(*args)


TILE = 256


def attend_body(groups, own, last, flags, q, *refs):
    refs = list(refs)
    count = sum(groups)
    kvs, refs = refs[:count], refs[count:]
    if not own:
        m_in, l_in, acc_in = refs[:3]
        refs = refs[3:]
    if last:
        out, m_s, l_s, acc_s = refs
    else:
        m_s, l_s, acc_s = refs
    rows, part = q.shape
    heads = part // HD
    factor = HD ** (-0.5) * math.log2(math.e)
    if not own:
        m_s[...] = m_in[...]
        l_s[...] = l_in[...]
        acc_s[...] = acc_in[...]

    def step(pieces, h, r, first):
        query = q[r : r + TILE, h * HD : (h + 1) * HD]
        scores, top = [], None
        for ref in pieces:
            keys = r + TILE if first else ref.shape[0]
            s = lax.dot_general(
                query,
                ref[0:keys, h * HD : (h + 1) * HD],
                (((1,), (1,)), ((), ())),
                preferred_element_type=F32,
            )
            if first:
                qpos = r + lax.broadcasted_iota(jnp.int32, s.shape, 0)
                kpos = lax.broadcasted_iota(jnp.int32, s.shape, 1)
                s = jnp.where(kpos <= qpos, s, -1e30)
            scores.append(s)
            for c in range(0, keys, 128):
                piece = s[:, c : c + 128]
                top = piece if top is None else jnp.maximum(top, piece)
        top = jnp.max(top, axis=1, keepdims=True) * factor
        if first:
            new = top
        else:
            old = m_s[h, r : r + TILE]
            new = jnp.maximum(old, top)
        total, mixed = None, None
        for ref, s in zip(pieces, scores, strict=True):
            keys = s.shape[1]
            e = jnp.exp2(s * factor - new)
            for c in range(0, keys, 128):
                piece = e[:, c : c + 128]
                total = piece if total is None else total + piece
            value = ref[0:keys, part + h * HD : part + (h + 1) * HD]
            term = jnp.dot(e.astype(BF), value, preferred_element_type=F32)
            mixed = term if mixed is None else mixed + term
        if first:
            l_s[h, r : r + TILE] = total
            acc_s[h, r : r + TILE] = mixed
        else:
            fade = jnp.exp2(old - new)
            l_s[h, r : r + TILE] = l_s[h, r : r + TILE] * fade + total
            acc_s[h, r : r + TILE] = acc_s[h, r : r + TILE] * fade + mixed
        m_s[h, r : r + TILE] = new

    at = 0
    for i, n in enumerate(groups):
        pieces = kvs[at : at + n]
        at += n

        def whole(pieces=pieces, first=own and i == 0):
            for h in range(heads):
                for r in range(0, rows, TILE):
                    step(pieces, h, r, first)

        if own and i == 0:
            whole()
        else:
            pl.when(flags[i] == 1)(whole)
    if last:
        for h in range(heads):
            total = jnp.sum(l_s[h], axis=1, keepdims=True)
            out[:, h * HD : (h + 1) * HD] = (acc_s[h] / total).astype(BF)


def attend(flags, q, groups, state, last):
    rows, width = q.shape
    heads = width // HD
    vmem = pl.BlockSpec(memory_space=pltpu.VMEM)
    state_shapes = [(heads, rows, 1), (heads, rows, 128), (heads, rows, HD)]
    pieces = [piece for group in groups for piece in group]
    counts = [len(group) for group in groups]
    args = [flags, q, *pieces] + (list(state) if state else [])
    if last:
        out_shape = jax.ShapeDtypeStruct((rows, width), BF)
        out_specs = vmem
        scratch = [pltpu.VMEM(shape, F32) for shape in state_shapes]
    else:
        out_shape = [jax.ShapeDtypeStruct(shape, F32) for shape in state_shapes]
        out_specs = [vmem] * 3
        scratch = []
    keys = sum(piece.shape[0] for piece in pieces)

    def body(*refs):
        attend_body(counts, state is None, last, *refs)

    return pl.pallas_call(
        body,
        in_specs=[pl.BlockSpec(memory_space=pltpu.SMEM)] + [vmem] * (len(args) - 1),
        out_specs=out_specs,
        out_shape=out_shape,
        scratch_shapes=scratch,
        compiler_params=params(24),
        cost_estimate=pl.CostEstimate(
            flops=4 * rows * keys * width,
            transcendentals=heads * rows * keys,
            bytes_accessed=4 * keys * width,
        ),
        name="attend",
    )(*args)


def on_device(features, se_filter, mr_filter, stream, w_out, norm_gain, w_qkv):
    rows, _, cols = features.shape
    feats = jnp.transpose(features, (1, 0, 2))
    taps = jnp.transpose(se_filter, (1, 0, 2))
    weights = jnp.transpose(w_qkv, (1, 0, 2))
    tensor_rank = lax.axis_index("tensor")
    context_rank = lax.axis_index("context")
    rank = tensor_rank.astype(jnp.int32).reshape(1)

    edge = jnp.concatenate(
        [feats[0, rows - 16 :], feats[1, rows - HALO :], feats[2, rows - HALO :]], axis=0
    )
    halo = lax.ppermute(edge, "context", [(c, c + 1) for c in range(2 * SIDE - 1)])
    gated = filters(feats, halo, taps, toeplitz(mr_filter))

    a, b = project(rank, gated, w_out)
    along_x = lambda v, d: hop(v, d, 0)
    along_y = lambda v, d: hop(v, 0, d)
    half = rows // 2
    own_a = (reduce_half(a, along_x, along_y) + stream[:half].astype(F32)).astype(BF)
    own_b = (reduce_half(b, along_y, along_x) + stream[half:].astype(F32)).astype(BF)
    stream_out = jnp.concatenate([own_a, own_b], axis=0)
    gain = norm_gain.reshape(GRID, cols)
    block_a, back_a, ahead_a = gather_line(own_a, along_y, along_x)
    block_b, back_b, ahead_b = gather_line(own_b, along_x, along_y)

    def pieces(a_blocks, b_blocks):
        out = [(v, [(far, d) for d in line], 0) for v, line, far in a_blocks]
        return out + [(v, [(d, far) for d in line], half) for v, line, far in b_blocks]

    near = pieces([(block_a, LINE, 0)], [(block_b, LINE, 0)])
    acc = qkv_part(rank, weights, gain, near, None, False)
    last_a = gather_rest(back_a, ahead_a, acc, along_x)
    last_b = gather_rest(back_b, ahead_b, acc, along_y)
    middle = pieces(
        [(back_a, LINE, 3), (ahead_a, LINE, 1)], [(back_b, LINE, 3), (ahead_b, LINE, 1)]
    )
    acc = qkv_part(rank, weights, gain, middle, acc, False)
    last = pieces(
        [(last_a[0], LINE[:2], 2), (last_a[1], LINE[2:], 2)],
        [(last_b[0], LINE[:2], 2), (last_b[1], LINE[2:], 2)],
    )
    query, kv = qkv_part(rank, weights, gain, last, acc, True)

    h = rows // 2
    z, core = context_rank // 2, context_rank % 2
    low, high = kv[:h], kv[h:]
    up = ((0, 1), (1, 2), (2, 3))
    down = ((0, 3), (1, 0))
    back_low, ahead_high = hop_z(low, up), hop_z(high, down)
    back_high, ahead_low = hop_z(high, up), hop_z(low, down)
    far_low = hop_z(back_low, ((1, 2), (2, 3)))
    far_high = hop_z(ahead_high, ((3, 2), (0, 3)))
    state = attend(
        jnp.stack([jnp.int32(1), (core == 1).astype(jnp.int32)]),
        query,
        [[kv], [swap_core(kv)]],
        None,
        False,
    )
    groups = [[back_low, back_high], [ahead_low, ahead_high], [far_low, far_high]]
    groups = [group + [swap_core(v) for v in group] for group in groups]
    flags = jnp.stack([((z + d) % SIDE < z).astype(jnp.int32) for d in (3, 1, 2)])
    context_out = attend(flags, query, groups, state, True)
    return stream_out, context_out


def solution(mesh):
    placed = (
        P("context", None, "tensor"),
        P(None, None, "tensor"),
        P(None, "tensor"),
        P("context", "tensor"),
        P("tensor", None),
        P(),
        P(None, None, "tensor"),
    )
    return jax.shard_map(
        on_device,
        mesh=mesh,
        in_specs=placed,
        out_specs=(P("context", "tensor"), P("context", "tensor")),
        check_vma=False,
    )
```

```python
import math

import jax
import jax.numpy as jnp
from jax import lax
from jax.experimental import pallas as pl
from jax.experimental.pallas import tpu as pltpu
from jax.sharding import PartitionSpec as P

HD = 128
SIDE = 4
GRID = 16
HALO = 144
BF = jnp.bfloat16
F32 = jnp.float32


def params(mib):
    return pltpu.CompilerParams(vmem_limit_bytes=mib * 1024 * 1024)


def hop(value, dx, dy):
    pairs = []
    for x in range(SIDE):
        for y in range(SIDE):
            pairs.append((x * SIDE + y, ((x + dx) % SIDE) * SIDE + (y + dy) % SIDE))
    return lax.ppermute(value, "tensor", pairs)


def hop_z(value, steps):
    pairs = [(z * 2 + core, to * 2 + core) for z, to in steps for core in range(2)]
    return lax.ppermute(value, "context", pairs)


def swap_core(value):
    return lax.ppermute(value, "context", [(c, c ^ 1) for c in range(2 * SIDE)])


def toeplitz_body(taps, out):
    for g in range(taps.shape[0]):
        row = jnp.broadcast_to(taps[g : g + 1, :], (128, 256))
        out[g] = pltpu.roll(row, 1, 1, stride=1, stride_axis=0).astype(BF)


def toeplitz(mr_filter):
    groups = mr_filter.shape[1]
    taps = jnp.pad(mr_filter[::-1].T.astype(F32), ((0, 0), (0, 128)))
    return pl.pallas_call(
        toeplitz_body,
        grid=(groups // 8,),
        in_specs=[pl.BlockSpec((8, 256), lambda i: (i, 0))],
        out_specs=pl.BlockSpec((8, 128, 256), lambda i: (i, 0, 0)),
        out_shape=jax.ShapeDtypeStruct((groups, 128, 256), BF),
        compiler_params=params(16),
        name="toeplitz",
    )(taps)


def filters_half(x0, x1, x2, taps, toep, kvs, block, store):
    width = taps.shape[1]
    lanes = slice(block * 128, (block + 1) * 128)

    def short(ref, j, start):
        total = taps[j, 0:1, lanes] * ref[start : start + 128]
        for s in range(1, width):
            total = total + taps[j, s : s + 1, lanes] * ref[start - s : start - s + 128]
        return total

    for b in range(3):
        start = HALO - 128 + b * 128
        kvs[b * 128 : (b + 1) * 128] = (short(x1, 1, start) * short(x2, 2, start)).astype(BF)
    lane_group = lax.broadcasted_iota(jnp.int32, (128, 128), 1) // 16
    lhs = toep[block * 8 : (block + 1) * 8].reshape(8 * 128, 256)
    for b in range(2):
        full = jnp.dot(lhs, kvs[b * 128 : b * 128 + 256], preferred_element_type=F32)
        medium = full[0:128]
        for g in range(1, 8):
            medium = jnp.where(lane_group == g, full[g * 128 : (g + 1) * 128], medium)
        store(b, (short(x0, 0, 16 + b * 128) * medium).astype(BF))


def piece_of(far, near):
    if far == 0:
        return "0", near
    if far == 2:
        return ("p", near) if near < 2 else ("m", near - 2)
    if far == 1:
        return ("1a", near) if near < 2 else ("p", near)
    return ("m", near + 2) if near < 2 else ("3b", near - 2)


def block_fetches(rank, names, swapped, w_hbm, wbuf, wsem):
    x, y = rank[0] // SIDE, rank[0] % SIDE
    cols = wbuf.shape[2]
    jobs = []
    for far in (2, 1, 3, 0):
        for near in range(SIDE):
            name, place = piece_of(far, near)
            if name not in names:
                continue
            dx, dy = (near, far) if swapped else (far, near)
            index = lax.rem(x + dx, SIDE) * SIDE + lax.rem(y + dy, SIDE)
            i = len(jobs)
            copy = pltpu.make_async_copy(
                w_hbm.at[:, pl.ds(pl.multiple_of(index * cols, cols), cols)],
                wbuf.at[i],
                wsem.at[i],
            )
            copy.start()
            jobs.append((copy, name, place))
    return jobs


def project_blocks(jobs, gated, wbuf, outs):
    for i, (copy, name, place) in enumerate(jobs):
        copy.wait()
        outs[name][place] = jnp.dot(gated[...], wbuf[i], preferred_element_type=F32).astype(BF)


def first_body(swapped, rank, feats, *refs):
    refs = list(refs)
    halo = None if swapped else refs.pop(0)
    taps, toep, w_hbm, gated, p, m, x0, x1, x2, kvs, wbuf, wsem = refs
    jobs = block_fetches(rank, ("p", "m"), swapped, w_hbm, wbuf, wsem)
    for block in range(feats.shape[2] // 128):
        lanes = slice(block * 128, (block + 1) * 128)
        if swapped:
            x0[...] = feats[0, 240:512, lanes].astype(F32)
            x1[...] = feats[1, 112:512, lanes].astype(F32)
            x2[...] = feats[2, 112:512, lanes].astype(F32)
        else:
            x0[0:16] = halo[0:16, lanes].astype(F32)
            x0[16:] = feats[0, 0:256, lanes].astype(F32)
            x1[0:HALO] = halo[16 : 16 + HALO, lanes].astype(F32)
            x1[HALO:] = feats[1, 0:256, lanes].astype(F32)
            x2[0:HALO] = halo[16 + HALO : 16 + 2 * HALO, lanes].astype(F32)
            x2[HALO:] = feats[2, 0:256, lanes].astype(F32)

        def store(b, value, lanes=lanes):
            gated[b * 128 : (b + 1) * 128, lanes] = value

        filters_half(x0, x1, x2, taps, toep, kvs, block, store)
    project_blocks(jobs, gated, wbuf, {"p": p, "m": m})


def first(rank, feats, halo, taps, toep, w_out):
    half, cols = feats.shape[1] // 2, feats.shape[2]
    swapped = halo is None
    vmem = pl.BlockSpec(memory_space=pltpu.VMEM)
    smem = pl.BlockSpec(memory_space=pltpu.SMEM)
    hbm = pl.BlockSpec(memory_space=pl.ANY)
    args = [rank, feats] + ([] if swapped else [halo]) + [taps, toep, w_out]
    block = jax.ShapeDtypeStruct((4, half, cols), BF)

    def body(*refs):
        first_body(swapped, *refs)

    return pl.pallas_call(
        body,
        in_specs=[smem] + [vmem] * (len(args) - 2) + [hbm],
        out_specs=[vmem] * 3,
        out_shape=[jax.ShapeDtypeStruct((half, cols), BF), block, block],
        scratch_shapes=[
            pltpu.VMEM((half + 16, 128), F32),
            pltpu.VMEM((half + HALO, 128), F32),
            pltpu.VMEM((half + HALO, 128), F32),
            pltpu.VMEM((half + 128, 128), BF),
            pltpu.VMEM((8, cols, cols), BF),
            pltpu.SemaphoreType.DMA((8,)),
        ],
        compiler_params=params(20),
        cost_estimate=pl.CostEstimate(
            flops=4 * 10**9, transcendentals=0, bytes_accessed=w_out.size
        ),
        name="first",
    )(*args)


def rest_body(swapped, rank, gated, w_hbm, p1a, p3b, p0, wbuf, wsem):
    jobs = block_fetches(rank, ("1a", "3b", "0"), swapped, w_hbm, wbuf, wsem)
    project_blocks(jobs, gated, wbuf, {"1a": p1a, "3b": p3b, "0": p0})


def rest(rank, gated, w_out, swapped):
    half, cols = gated.shape
    vmem = pl.BlockSpec(memory_space=pltpu.VMEM)

    def body(*refs):
        rest_body(swapped, *refs)

    return pl.pallas_call(
        body,
        in_specs=[
            pl.BlockSpec(memory_space=pltpu.SMEM),
            vmem,
            pl.BlockSpec(memory_space=pl.ANY),
        ],
        out_specs=[vmem] * 3,
        out_shape=[jax.ShapeDtypeStruct((n, half, cols), BF) for n in (2, 2, 4)],
        scratch_shapes=[pltpu.VMEM((8, cols, cols), BF), pltpu.SemaphoreType.DMA((8,))],
        compiler_params=params(12),
        cost_estimate=pl.CostEstimate(
            flops=half * w_out.size, transcendentals=0, bytes_accessed=w_out.size
        ),
        name="rest",
    )(rank, gated, w_out)


def plus(*terms):
    total = terms[0].astype(F32)
    for term in terms[1:]:
        total = total + term.astype(F32)
    return total


def reduce_line(p, send):
    rp = send(p["p"], 1)
    rm = send(p["m"], -1)
    r1a = send(plus(p["1a"], rp[0:2]).astype(BF), 1)
    r3b = send(plus(p["3b"], rm[0:2]).astype(BF), -1)
    low = plus(p["0"][0:2], rm[2:4], r1a)
    high = plus(p["0"][2:4], rp[2:4], r3b)
    return low[0], low[1], high[0], high[1]


def messages(blocks):
    _, one, two, three = blocks
    h = one.shape[0] // 2
    up = jnp.concatenate([two[:h], one[h:]], axis=0).astype(BF)
    down = jnp.concatenate([two[h:], three[:h]], axis=0).astype(BF)
    return up, down


def reduce_rest(blocks, sp, sm, send):
    mine, one, _, three = blocks
    h = one.shape[0] // 2
    s1a = send(plus(one[:h], sp[:h]).astype(BF), 1)
    s3b = send(plus(three[h:], sm[:h]).astype(BF), -1)
    return plus(mine, jnp.concatenate([s1a, s3b], axis=0), jnp.concatenate([sm[h:], sp[h:]], axis=0))


def gather_line(own, first, second):
    h = own.shape[0] // 2
    back = first(own, 1)
    ahead = first(own, -1)
    far = jnp.concatenate([first(back[:h], 1), first(ahead[h:], -1)], axis=0)
    one = jnp.stack([own, back])
    two = jnp.stack([ahead, far])
    received = second(one, 1), second(one, -1), second(two, 1), second(two, -1)
    return one, two, received


def qkv_body(spec, has_acc, last, rank, w, gain, *refs):
    refs = list(refs)
    acc_in = refs.pop(0) if has_acc else None
    count = len(spec)
    pieces, refs = refs[:count], refs[count:]
    if last:
        q_out, kv_out, acc, xbuf = refs
    else:
        acc, xbuf = refs
    x, y = rank[0] // SIDE, rank[0] % SIDE
    part = w.shape[2]
    depth = gain.shape[1]
    filled = set()
    for (places, row), ref in zip(spec, pieces, strict=True):
        total = None
        rows = pl.ds(row, ref.shape[1])
        starts = []
        for k, place in enumerate(places):
            index = lax.rem(x + place[0], SIDE) * SIDE + lax.rem(y + place[1], SIDE)
            starts.append(pl.multiple_of(index * depth, depth))
            value = ref[k].astype(F32)
            for c in range(0, depth, 128):
                square = value[:, c : c + 128] * value[:, c : c + 128]
                total = square if total is None else total + square
            xbuf[k] = (value * gain[pl.ds(index, 1), :]).astype(BF)
        before = acc if row in filled else acc_in
        filled.add(row)
        for j in range(3):
            cols = slice(j * part, (j + 1) * part)
            term = None if before is None else before[rows, cols]
            for k, start in enumerate(starts):
                product = jnp.dot(
                    xbuf[k], w[j, pl.ds(start, depth), :], preferred_element_type=F32
                )
                term = product if term is None else term + product
            acc[rows, cols] = term
        acc[rows, 3 * part :] = total if before is None else before[rows, 3 * part :] + total
    if last:
        mean = jnp.sum(acc[:, 3 * part :], axis=1, keepdims=True) / (depth * GRID)
        scale = lax.rsqrt(mean + 1e-05)
        kv_out[...] = (acc[:, part : 3 * part] * scale).astype(BF)
        q_out[...] = (acc[:, :part] * scale).astype(BF)


def qkv_part(rank, w, gain, pieces, acc, last):
    spec = [(places, row) for _, places, row in pieces]
    part = w.shape[2]
    half, depth = pieces[0][0].shape[1:]
    rows = 2 * half
    vmem = pl.BlockSpec(memory_space=pltpu.VMEM)
    args = [rank, w, gain]
    specs = [pl.BlockSpec(memory_space=pltpu.SMEM), vmem, vmem]
    if acc is not None:
        args.append(acc)
        specs.append(vmem)
    for piece in pieces:
        args.append(piece[0])
        specs.append(vmem)
    scratch = [pltpu.VMEM((4, half, depth), BF)]
    acc_shape = (rows, 3 * part + 128)
    if last:
        out_shape = [
            jax.ShapeDtypeStruct((rows, part), BF),
            jax.ShapeDtypeStruct((rows, 2 * part), BF),
        ]
        out_specs = [vmem, vmem]
        scratch = [pltpu.VMEM(acc_shape, F32)] + scratch
    else:
        out_shape = jax.ShapeDtypeStruct(acc_shape, F32)
        out_specs = vmem

    def body(*refs):
        qkv_body(spec, acc is not None, last, *refs)

    blocks = sum(len(places) for places, _ in spec)
    return pl.pallas_call(
        body,
        in_specs=specs,
        out_specs=out_specs,
        out_shape=out_shape,
        scratch_shapes=scratch,
        compiler_params=params(24),
        cost_estimate=pl.CostEstimate(
            flops=blocks * 2 * half * depth * 3 * part,
            transcendentals=0,
            bytes_accessed=blocks * 6 * depth * part,
        ),
        name="qkv",
    )(*args)


TILE = 256


def attend_body(groups, shifts, own, last, rank, q, *refs):
    refs = list(refs)
    count = sum(groups)
    kvs, refs = refs[:count], refs[count:]
    if not own:
        m_in, l_in, acc_in = refs[:3]
        refs = refs[3:]
    if last:
        out, m_s, l_s, acc_s = refs
    else:
        m_s, l_s, acc_s = refs
    rows, part = q.shape
    heads = part // HD
    factor = HD ** (-0.5) * math.log2(math.e)
    if not own:
        m_s[...] = m_in[...]
        l_s[...] = l_in[...]
        acc_s[...] = acc_in[...]

    def step(pieces, h, r, first):
        query = q[r : r + TILE, h * HD : (h + 1) * HD]
        scores, top = [], None
        for ref in pieces:
            keys = r + TILE if first else ref.shape[0]
            s = lax.dot_general(
                query,
                ref[0:keys, h * HD : (h + 1) * HD],
                (((1,), (1,)), ((), ())),
                preferred_element_type=F32,
            )
            if first:
                qpos = r + lax.broadcasted_iota(jnp.int32, s.shape, 0)
                kpos = lax.broadcasted_iota(jnp.int32, s.shape, 1)
                s = jnp.where(kpos <= qpos, s, -1e30)
            scores.append(s)
            for c in range(0, keys, 128):
                piece = s[:, c : c + 128]
                top = piece if top is None else jnp.maximum(top, piece)
        top = jnp.max(top, axis=1, keepdims=True) * factor
        if first:
            new = top
        else:
            old = m_s[h, r : r + TILE]
            new = jnp.maximum(old, top)
        total, mixed = None, None
        for ref, s in zip(pieces, scores, strict=True):
            keys = s.shape[1]
            e = jnp.exp2(s * factor - new)
            for c in range(0, keys, 128):
                piece = e[:, c : c + 128]
                total = piece if total is None else total + piece
            value = ref[0:keys, part + h * HD : part + (h + 1) * HD]
            term = jnp.dot(e.astype(BF), value, preferred_element_type=F32)
            mixed = term if mixed is None else mixed + term
        if first:
            l_s[h, r : r + TILE] = total
            acc_s[h, r : r + TILE] = mixed
        else:
            fade = jnp.exp2(old - new)
            l_s[h, r : r + TILE] = l_s[h, r : r + TILE] * fade + total
            acc_s[h, r : r + TILE] = acc_s[h, r : r + TILE] * fade + mixed
        m_s[h, r : r + TILE] = new

    at = 0
    for i, n in enumerate(groups):
        pieces = kvs[at : at + n]
        at += n

        def whole(pieces=pieces, first=own and i == 0):
            for h in range(heads):
                for r in range(0, rows, TILE):
                    step(pieces, h, r, first)

        if own and i == 0:
            whole()
        else:
            z, core = rank[0] // 2, rank[0] % 2
            shift = shifts[i]
            pl.when(core == 1 if shift == 0 else lax.rem(z + shift, SIDE) < z)(whole)
    if last:
        for h in range(heads):
            total = jnp.sum(l_s[h], axis=1, keepdims=True)
            out[:, h * HD : (h + 1) * HD] = (acc_s[h] / total).astype(BF)


def attend(rank, q, groups, shifts, state, last):
    rows, width = q.shape
    heads = width // HD
    vmem = pl.BlockSpec(memory_space=pltpu.VMEM)
    state_shapes = [(heads, rows, 1), (heads, rows, 128), (heads, rows, HD)]
    pieces = [piece for group in groups for piece in group]
    counts = [len(group) for group in groups]
    args = [rank, q, *pieces] + (list(state) if state else [])
    if last:
        out_shape = jax.ShapeDtypeStruct((rows, width), BF)
        out_specs = vmem
        scratch = [pltpu.VMEM(shape, F32) for shape in state_shapes]
    else:
        out_shape = [jax.ShapeDtypeStruct(shape, F32) for shape in state_shapes]
        out_specs = [vmem] * 3
        scratch = []
    keys = sum(piece.shape[0] for piece in pieces)

    def body(*refs):
        attend_body(counts, shifts, state is None, last, *refs)

    return pl.pallas_call(
        body,
        in_specs=[pl.BlockSpec(memory_space=pltpu.SMEM)] + [vmem] * (len(args) - 1),
        out_specs=out_specs,
        out_shape=out_shape,
        scratch_shapes=scratch,
        compiler_params=params(24),
        cost_estimate=pl.CostEstimate(
            flops=4 * rows * keys * width,
            transcendentals=heads * rows * keys,
            bytes_accessed=4 * keys * width,
        ),
        name="attend",
    )(*args)


def on_device(features, se_filter, mr_filter, stream, w_out, norm_gain, w_qkv):
    rows, _, cols = features.shape
    feats = jnp.transpose(features, (1, 0, 2))
    taps = jnp.transpose(se_filter, (1, 0, 2))
    weights = jnp.transpose(w_qkv, (1, 0, 2))
    tensor_rank = lax.axis_index("tensor")
    context_rank = lax.axis_index("context")
    rank = tensor_rank.astype(jnp.int32).reshape(1)

    edge = jnp.concatenate(
        [feats[0, rows - 16 :], feats[1, rows - HALO :], feats[2, rows - HALO :]], axis=0
    )
    halo = lax.ppermute(edge, "context", [(c, c + 1) for c in range(2 * SIDE - 1)])
    toep = toeplitz(mr_filter)
    w_out = pltpu.with_memory_space_constraint(w_out, pltpu.HBM)
    blocks = {}
    for swapped in (True, False):
        gated, p, m = first(rank, feats, None if swapped else halo, taps, toep, w_out)
        blocks[swapped] = (gated, p, m)
    sums = {}
    for swapped in (True, False):
        gated, p, m = blocks[swapped]
        p1a, p3b, p0 = rest(rank, gated, w_out, swapped)
        sums[swapped] = {"p": p, "m": m, "1a": p1a, "3b": p3b, "0": p0}
    along_x = lambda v, d: hop(v, d, 0)
    along_y = lambda v, d: hop(v, 0, d)
    half = rows // 2
    blocks_b = reduce_line(sums[True], along_y)
    blocks_a = reduce_line(sums[False], along_x)
    up_b, down_b = messages(blocks_b)
    sp_b, sm_b = along_x(up_b, 1), along_x(down_b, -1)
    up_a, down_a = messages(blocks_a)
    sp_a, sm_a = along_y(up_a, 1), along_y(down_a, -1)
    sp_b, sm_b, _, _ = lax.optimization_barrier((sp_b, sm_b, up_a, down_a))
    own_b = (reduce_rest(blocks_b, sp_b, sm_b, along_x) + stream[half:].astype(F32)).astype(BF)
    own_a = (reduce_rest(blocks_a, sp_a, sm_a, along_y) + stream[:half].astype(F32)).astype(BF)
    stream_out = jnp.concatenate([own_a, own_b], axis=0)
    gain = norm_gain.reshape(GRID, cols)
    ones, twos = (0, 3), (1, 2)
    one_a, two_a, got_a = gather_line(own_a, along_y, along_x)
    one_b, two_b, got_b = gather_line(own_b, along_x, along_y)

    def pieces(a_blocks, b_blocks):
        out = [(v, [(far, d) for d in line], 0) for v, line, far in a_blocks]
        return out + [(v, [(d, far) for d in line], half) for v, line, far in b_blocks]

    near = pieces([(one_a, ones, 0), (two_a, twos, 0)], [(one_b, ones, 0), (two_b, twos, 0)])
    acc = qkv_part(rank, weights, gain, near, None, False)
    middle, last = [], []
    for got, second in ((got_a, along_x), (got_b, along_y)):
        end, _ = lax.optimization_barrier((got[3], acc))
        middle.append([(got[0], ones, 3), (got[1], ones, 1), (got[2], twos, 3), (got[3], twos, 1)])
        last.append([(second(got[0], 1), ones, 2), (second(end, -1), twos, 2)])
    acc = qkv_part(rank, weights, gain, pieces(*middle), acc, False)
    query, kv = qkv_part(rank, weights, gain, pieces(*last), acc, True)

    h = rows // 2
    place = context_rank.astype(jnp.int32).reshape(1)
    back = hop_z(kv, ((0, 1), (1, 2), (2, 3)))
    ahead = hop_z(kv, ((0, 3), (1, 0)))
    state = attend(place, query, [[kv], [swap_core(kv)]], (0, 0), None, False)
    back, ahead, state = lax.optimization_barrier((back, ahead, state))
    far_low = hop_z(back[:h], ((1, 2), (2, 3)))
    far_high = hop_z(ahead[h:], ((3, 2), (0, 3)))
    groups = [[back, swap_core(back)], [ahead, swap_core(ahead)]]
    state = attend(place, query, groups, (3, 1), state, False)
    far_low, far_high, state = lax.optimization_barrier((far_low, far_high, state))
    groups = [[far_low, far_high, swap_core(far_low), swap_core(far_high)]]
    context_out = attend(place, query, groups, (2,), state, True)
    return stream_out, context_out


def solution(mesh):
    placed = (
        P("context", None, "tensor"),
        P(None, None, "tensor"),
        P(None, "tensor"),
        P("context", "tensor"),
        P("tensor", None),
        P(),
        P(None, None, "tensor"),
    )
    return jax.shard_map(
        on_device,
        mesh=mesh,
        in_specs=placed,
        out_specs=(P("context", "tensor"), P("context", "tensor")),
        check_vma=False,
    )
```

```python
import math

import jax
import jax.numpy as jnp
from jax import lax
from jax.experimental import pallas as pl
from jax.experimental.pallas import tpu as pltpu
from jax.sharding import PartitionSpec as P

HD = 128
SIDE = 4
GRID = 16
HALO = 144
BF = jnp.bfloat16
F32 = jnp.float32


def params(mib):
    return pltpu.CompilerParams(vmem_limit_bytes=mib * 1024 * 1024)


def hop(value, dx, dy):
    pairs = []
    for x in range(SIDE):
        for y in range(SIDE):
            pairs.append((x * SIDE + y, ((x + dx) % SIDE) * SIDE + (y + dy) % SIDE))
    return lax.ppermute(value, "tensor", pairs)


def hop_z(value, steps):
    pairs = [(z * 2 + core, to * 2 + core) for z, to in steps for core in range(2)]
    return lax.ppermute(value, "context", pairs)


def swap_core(value):
    return lax.ppermute(value, "context", [(c, c ^ 1) for c in range(2 * SIDE)])


def toeplitz_body(taps, out):
    groups, width = taps.shape
    row = lax.broadcasted_iota(jnp.int32, (width, width), 0)
    col = lax.broadcasted_iota(jnp.int32, (width, width), 1)
    flip = (row + col == width - 1).astype(BF)
    reversed_taps = jnp.dot(taps[...], flip, preferred_element_type=F32)
    padded = jnp.concatenate([reversed_taps, jnp.zeros_like(reversed_taps)], axis=1)
    for g in range(groups):
        wide = jnp.broadcast_to(padded[g : g + 1, :], (width, 2 * width))
        out[g] = pltpu.roll(wide, 1, 1, stride=1, stride_axis=0).astype(BF)


def toeplitz(mr_filter):
    taps = mr_filter.T
    groups, width = taps.shape
    vmem = pl.BlockSpec(memory_space=pltpu.VMEM)
    return pl.pallas_call(
        toeplitz_body,
        in_specs=[vmem],
        out_specs=vmem,
        out_shape=jax.ShapeDtypeStruct((groups, width, 2 * width), BF),
        compiler_params=params(16),
        name="toeplitz",
    )(taps)


def fetch_body(source, out, sem):
    copy = pltpu.make_async_copy(source, out, sem)
    copy.start()
    copy.wait()


def fetch(source):
    return pl.pallas_call(
        fetch_body,
        in_specs=[pl.BlockSpec(memory_space=pl.ANY)],
        out_specs=pl.BlockSpec(memory_space=pltpu.VMEM),
        out_shape=jax.ShapeDtypeStruct(source.shape, source.dtype),
        scratch_shapes=[pltpu.SemaphoreType.DMA],
        compiler_params=params(16),
        name="fetch",
    )(pltpu.with_memory_space_constraint(source, pltpu.HBM))


def filters_half(x0, x1, x2, taps, toep, kvs, block, store):
    width = taps.shape[1]
    lanes = slice(block * 128, (block + 1) * 128)

    def short(ref, j, start):
        total = taps[j, 0:1, lanes] * ref[start : start + 128]
        for s in range(1, width):
            total = total + taps[j, s : s + 1, lanes] * ref[start - s : start - s + 128]
        return total

    for b in range(3):
        start = HALO - 128 + b * 128
        kvs[b * 128 : (b + 1) * 128] = (short(x1, 1, start) * short(x2, 2, start)).astype(BF)
    lane_group = lax.broadcasted_iota(jnp.int32, (128, 128), 1) // 16
    lhs = toep[block * 8 : (block + 1) * 8].reshape(8 * 128, 256)
    for b in range(2):
        full = jnp.dot(lhs, kvs[b * 128 : b * 128 + 256], preferred_element_type=F32)
        medium = full[0:128]
        for g in range(1, 8):
            medium = jnp.where(lane_group == g, full[g * 128 : (g + 1) * 128], medium)
        store(b, (short(x0, 0, 16 + b * 128) * medium).astype(BF))


def piece_of(far, near):
    if far == 0:
        return "0", near
    if far == 2:
        return ("p", near) if near < 2 else ("m", near - 2)
    if far == 1:
        return ("1a", near) if near < 2 else ("p", near)
    return ("m", near + 2) if near < 2 else ("3b", near - 2)


def block_fetches(rank, names, swapped, w_hbm, wbuf, wsem):
    x, y = rank[0] // SIDE, rank[0] % SIDE
    cols = wbuf.shape[2]
    jobs = []
    for far in (2, 1, 3, 0):
        for near in range(SIDE):
            name, place = piece_of(far, near)
            if name not in names:
                continue
            dx, dy = (near, far) if swapped else (far, near)
            index = lax.rem(x + dx, SIDE) * SIDE + lax.rem(y + dy, SIDE)
            i = len(jobs)
            copy = pltpu.make_async_copy(
                w_hbm.at[:, pl.ds(pl.multiple_of(index * cols, cols), cols)],
                wbuf.at[i],
                wsem.at[i],
            )
            copy.start()
            jobs.append((copy, name, place))
    return jobs


def project_blocks(jobs, gated, wbuf, outs):
    for i, (copy, name, place) in enumerate(jobs):
        copy.wait()
        outs[name][place] = jnp.dot(gated[...], wbuf[i], preferred_element_type=F32).astype(BF)


def first_body(swapped, rank, feats, *refs):
    refs = list(refs)
    halo = None if swapped else refs.pop(0)
    taps, toep, w_hbm, gated, p, m, x0, x1, x2, kvs, wbuf, wsem = refs
    jobs = block_fetches(rank, ("p", "m"), swapped, w_hbm, wbuf, wsem)
    for block in range(feats.shape[2] // 128):
        lanes = slice(block * 128, (block + 1) * 128)
        if swapped:
            x0[...] = feats[0, 240:512, lanes].astype(F32)
            x1[...] = feats[1, 112:512, lanes].astype(F32)
            x2[...] = feats[2, 112:512, lanes].astype(F32)
        else:
            x0[0:16] = halo[0, HALO - 16 :, lanes].astype(F32)
            x0[16:] = feats[0, 0:256, lanes].astype(F32)
            x1[0:HALO] = halo[1, :, lanes].astype(F32)
            x1[HALO:] = feats[1, 0:256, lanes].astype(F32)
            x2[0:HALO] = halo[2, :, lanes].astype(F32)
            x2[HALO:] = feats[2, 0:256, lanes].astype(F32)

        def store(b, value, lanes=lanes):
            gated[b * 128 : (b + 1) * 128, lanes] = value

        filters_half(x0, x1, x2, taps, toep, kvs, block, store)
    project_blocks(jobs, gated, wbuf, {"p": p, "m": m})


def first(rank, feats, halo, taps, toep, w_out):
    half, cols = feats.shape[1] // 2, feats.shape[2]
    swapped = halo is None
    vmem = pl.BlockSpec(memory_space=pltpu.VMEM)
    smem = pl.BlockSpec(memory_space=pltpu.SMEM)
    hbm = pl.BlockSpec(memory_space=pl.ANY)
    args = [rank, feats] + ([] if swapped else [halo]) + [taps, toep, w_out]
    block = jax.ShapeDtypeStruct((4, half, cols), BF)

    def body(*refs):
        first_body(swapped, *refs)

    return pl.pallas_call(
        body,
        in_specs=[smem] + [vmem] * (len(args) - 2) + [hbm],
        out_specs=[vmem] * 3,
        out_shape=[jax.ShapeDtypeStruct((half, cols), BF), block, block],
        scratch_shapes=[
            pltpu.VMEM((half + 16, 128), F32),
            pltpu.VMEM((half + HALO, 128), F32),
            pltpu.VMEM((half + HALO, 128), F32),
            pltpu.VMEM((half + 128, 128), BF),
            pltpu.VMEM((8, cols, cols), BF),
            pltpu.SemaphoreType.DMA((8,)),
        ],
        compiler_params=params(20),
        cost_estimate=pl.CostEstimate(
            flops=4 * 10**9, transcendentals=0, bytes_accessed=w_out.size
        ),
        name="first",
    )(*args)


def rest_body(swapped, rank, gated, w_hbm, p1a, p3b, p0, wbuf, wsem):
    jobs = block_fetches(rank, ("1a", "3b", "0"), swapped, w_hbm, wbuf, wsem)
    project_blocks(jobs, gated, wbuf, {"1a": p1a, "3b": p3b, "0": p0})


def rest(rank, gated, w_out, swapped):
    half, cols = gated.shape
    vmem = pl.BlockSpec(memory_space=pltpu.VMEM)

    def body(*refs):
        rest_body(swapped, *refs)

    return pl.pallas_call(
        body,
        in_specs=[
            pl.BlockSpec(memory_space=pltpu.SMEM),
            vmem,
            pl.BlockSpec(memory_space=pl.ANY),
        ],
        out_specs=[vmem] * 3,
        out_shape=[jax.ShapeDtypeStruct((n, half, cols), BF) for n in (2, 2, 4)],
        scratch_shapes=[pltpu.VMEM((8, cols, cols), BF), pltpu.SemaphoreType.DMA((8,))],
        compiler_params=params(12),
        cost_estimate=pl.CostEstimate(
            flops=half * w_out.size, transcendentals=0, bytes_accessed=w_out.size
        ),
        name="rest",
    )(rank, gated, w_out)


def plus(*terms):
    total = terms[0].astype(F32)
    for term in terms[1:]:
        total = total + term.astype(F32)
    return total


def reduce_line(p, send):
    rp = send(p["p"], 1)
    rm = send(p["m"], -1)
    r1a = send(plus(p["1a"], rp[0:2]).astype(BF), 1)
    r3b = send(plus(p["3b"], rm[0:2]).astype(BF), -1)
    low = plus(p["0"][0:2], rm[2:4], r1a)
    high = plus(p["0"][2:4], rp[2:4], r3b)
    return low[0], low[1], high[0], high[1]


def messages(blocks):
    _, one, two, three = blocks
    h = one.shape[0] // 2
    up = jnp.concatenate([two[:h], one[h:]], axis=0).astype(BF)
    down = jnp.concatenate([two[h:], three[:h]], axis=0).astype(BF)
    return up, down


def reduce_rest(blocks, sp, sm, send):
    mine, one, _, three = blocks
    h = one.shape[0] // 2
    s1a = send(plus(one[:h], sp[:h]).astype(BF), 1)
    s3b = send(plus(three[h:], sm[:h]).astype(BF), -1)
    return plus(mine, jnp.concatenate([s1a, s3b], axis=0), jnp.concatenate([sm[h:], sp[h:]], axis=0))


def gather_line(own, first, second):
    h = own.shape[0] // 2
    back = first(own, 1)
    ahead = first(own, -1)
    far = jnp.concatenate([first(back[:h], 1), first(ahead[h:], -1)], axis=0)
    one = jnp.stack([own, back])
    two = jnp.stack([ahead, far])
    received = second(one, 1), second(one, -1), second(two, 1), second(two, -1)
    return one, two, received


def qkv_body(spec, has_acc, last, rank, w, gain, *refs):
    refs = list(refs)
    acc_in = refs.pop(0) if has_acc else None
    count = len(spec)
    pieces, refs = refs[:count], refs[count:]
    if last:
        q_out, kv_out, acc, xbuf = refs
    else:
        acc, xbuf = refs
    x, y = rank[0] // SIDE, rank[0] % SIDE
    part = w.shape[2]
    depth = gain.shape[1]
    filled = set()
    for (places, row), ref in zip(spec, pieces, strict=True):
        total = None
        rows = pl.ds(row, ref.shape[1])
        starts = []
        for k, place in enumerate(places):
            index = lax.rem(x + place[0], SIDE) * SIDE + lax.rem(y + place[1], SIDE)
            starts.append(pl.multiple_of(index * depth, depth))
            value = ref[k].astype(F32)
            for c in range(0, depth, 128):
                square = value[:, c : c + 128] * value[:, c : c + 128]
                total = square if total is None else total + square
            xbuf[k] = (value * gain[pl.ds(index, 1), :]).astype(BF)
        before = acc if row in filled else acc_in
        filled.add(row)
        for j in range(3):
            cols = slice(j * part, (j + 1) * part)
            term = None if before is None else before[rows, cols]
            for k, start in enumerate(starts):
                product = jnp.dot(
                    xbuf[k], w[j, pl.ds(start, depth), :], preferred_element_type=F32
                )
                term = product if term is None else term + product
            acc[rows, cols] = term
        acc[rows, 3 * part :] = total if before is None else before[rows, 3 * part :] + total
    if last:
        mean = jnp.sum(acc[:, 3 * part :], axis=1, keepdims=True) / (depth * GRID)
        scale = lax.rsqrt(mean + 1e-05)
        kv_out[...] = (acc[:, part : 3 * part] * scale).astype(BF)
        q_out[...] = (acc[:, :part] * scale).astype(BF)


def qkv_part(rank, w, gain, pieces, acc, last):
    spec = [(places, row) for _, places, row in pieces]
    part = w.shape[2]
    half, depth = pieces[0][0].shape[1:]
    rows = 2 * half
    vmem = pl.BlockSpec(memory_space=pltpu.VMEM)
    args = [rank, w, gain]
    specs = [pl.BlockSpec(memory_space=pltpu.SMEM), vmem, vmem]
    if acc is not None:
        args.append(acc)
        specs.append(vmem)
    for piece in pieces:
        args.append(piece[0])
        specs.append(vmem)
    scratch = [pltpu.VMEM((4, half, depth), BF)]
    acc_shape = (rows, 3 * part + 128)
    if last:
        out_shape = [
            jax.ShapeDtypeStruct((rows, part), BF),
            jax.ShapeDtypeStruct((rows, 2 * part), BF),
        ]
        out_specs = [vmem, vmem]
        scratch = [pltpu.VMEM(acc_shape, F32)] + scratch
    else:
        out_shape = jax.ShapeDtypeStruct(acc_shape, F32)
        out_specs = vmem

    def body(*refs):
        qkv_body(spec, acc is not None, last, *refs)

    blocks = sum(len(places) for places, _ in spec)
    return pl.pallas_call(
        body,
        in_specs=specs,
        out_specs=out_specs,
        out_shape=out_shape,
        scratch_shapes=scratch,
        compiler_params=params(24),
        cost_estimate=pl.CostEstimate(
            flops=blocks * 2 * half * depth * 3 * part,
            transcendentals=0,
            bytes_accessed=blocks * 6 * depth * part,
        ),
        name="qkv",
    )(*args)


TILE = 256


def attend_body(groups, shifts, own, last, rank, q, *refs):
    refs = list(refs)
    count = sum(groups)
    kvs, refs = refs[:count], refs[count:]
    if not own:
        m_in, l_in, acc_in = refs[:3]
        refs = refs[3:]
    if last:
        out, m_s, l_s, acc_s = refs
    else:
        m_s, l_s, acc_s = refs
    rows, part = q.shape
    heads = part // HD
    factor = HD ** (-0.5) * math.log2(math.e)
    if not own:
        m_s[...] = m_in[...]
        l_s[...] = l_in[...]
        acc_s[...] = acc_in[...]

    def score(pieces, h, r, first):
        query = q[r : r + TILE, h * HD : (h + 1) * HD]
        scores = []
        for ref in pieces:
            keys = r + TILE if first else ref.shape[0]
            s = lax.dot_general(
                query,
                ref[0:keys, h * HD : (h + 1) * HD],
                (((1,), (1,)), ((), ())),
                preferred_element_type=F32,
            )
            if first:
                qpos = r + lax.broadcasted_iota(jnp.int32, s.shape, 0)
                kpos = lax.broadcasted_iota(jnp.int32, s.shape, 1)
                s = jnp.where(kpos <= qpos, s, -1e30)
            scores.append(s)
        return scores

    def step(pieces, scores, h, r, first):
        top = None
        for s in scores:
            for c in range(0, s.shape[1], 128):
                piece = s[:, c : c + 128]
                top = piece if top is None else jnp.maximum(top, piece)
        top = jnp.max(top, axis=1, keepdims=True) * factor
        if first:
            new = top
        else:
            old = m_s[h, r : r + TILE]
            new = jnp.maximum(old, top)
        total, mixed = None, None
        for ref, s in zip(pieces, scores, strict=True):
            keys = s.shape[1]
            e = jnp.exp2(s * factor - new)
            for c in range(0, keys, 128):
                piece = e[:, c : c + 128]
                total = piece if total is None else total + piece
            value = ref[0:keys, part + h * HD : part + (h + 1) * HD]
            term = jnp.dot(e.astype(BF), value, preferred_element_type=F32)
            mixed = term if mixed is None else mixed + term
        if first:
            l_s[h, r : r + TILE] = total
            acc_s[h, r : r + TILE] = mixed
        else:
            fade = jnp.exp2(old - new)
            l_s[h, r : r + TILE] = l_s[h, r : r + TILE] * fade + total
            acc_s[h, r : r + TILE] = acc_s[h, r : r + TILE] * fade + mixed
        m_s[h, r : r + TILE] = new

    at = 0
    for i, n in enumerate(groups):
        pieces = kvs[at : at + n]
        at += n

        def whole(pieces=pieces, first=own and i == 0):
            tiles = [(h, r) for h in range(heads) for r in range(0, rows, TILE)]
            ready = [score(pieces, h, r, first) for h, r in tiles]
            for (h, r), scores in zip(tiles, ready, strict=True):
                step(pieces, scores, h, r, first)

        if own and i == 0:
            whole()
        else:
            z, core = rank[0] // 2, rank[0] % 2
            shift = shifts[i]
            pl.when(core == 1 if shift == 0 else lax.rem(z + shift, SIDE) < z)(whole)
    if last:
        for h in range(heads):
            total = jnp.sum(l_s[h], axis=1, keepdims=True)
            out[:, h * HD : (h + 1) * HD] = (acc_s[h] / total).astype(BF)


def attend(rank, q, groups, shifts, state, last):
    rows, width = q.shape
    heads = width // HD
    vmem = pl.BlockSpec(memory_space=pltpu.VMEM)
    state_shapes = [(heads, rows, 1), (heads, rows, 128), (heads, rows, HD)]
    pieces = [piece for group in groups for piece in group]
    counts = [len(group) for group in groups]
    args = [rank, q, *pieces] + (list(state) if state else [])
    if last:
        out_shape = jax.ShapeDtypeStruct((rows, width), BF)
        out_specs = vmem
        scratch = [pltpu.VMEM(shape, F32) for shape in state_shapes]
    else:
        out_shape = [jax.ShapeDtypeStruct(shape, F32) for shape in state_shapes]
        out_specs = [vmem] * 3
        scratch = []
    keys = sum(piece.shape[0] for piece in pieces)

    def body(*refs):
        attend_body(counts, shifts, state is None, last, *refs)

    return pl.pallas_call(
        body,
        in_specs=[pl.BlockSpec(memory_space=pltpu.SMEM)] + [vmem] * (len(args) - 1),
        out_specs=out_specs,
        out_shape=out_shape,
        scratch_shapes=scratch,
        compiler_params=params(24),
        cost_estimate=pl.CostEstimate(
            flops=4 * rows * keys * width,
            transcendentals=heads * rows * keys,
            bytes_accessed=4 * keys * width,
        ),
        name="attend",
    )(*args)


def on_device(features, se_filter, mr_filter, stream, w_out, norm_gain, w_qkv):
    rows, _, cols = features.shape
    feats = jnp.transpose(features, (1, 0, 2))
    taps = jnp.transpose(se_filter, (1, 0, 2))
    weights = jnp.transpose(w_qkv, (1, 0, 2))
    tensor_rank = lax.axis_index("tensor")
    context_rank = lax.axis_index("context")
    rank = tensor_rank.astype(jnp.int32).reshape(1)

    edge = feats[:, rows - HALO :]
    halo = lax.ppermute(edge, "context", [(c, c + 1) for c in range(2 * SIDE - 1)])
    toep = toeplitz(mr_filter)
    w_out = pltpu.with_memory_space_constraint(w_out, pltpu.HBM)
    blocks = {}
    for swapped in (True, False):
        gated, p, m = first(rank, feats, None if swapped else halo, taps, toep, w_out)
        blocks[swapped] = (gated, p, m)
    sums = {}
    for swapped in (True, False):
        gated, p, m = blocks[swapped]
        p1a, p3b, p0 = rest(rank, gated, w_out, swapped)
        sums[swapped] = {"p": p, "m": m, "1a": p1a, "3b": p3b, "0": p0}
    along_x = lambda v, d: hop(v, d, 0)
    along_y = lambda v, d: hop(v, 0, d)
    half = rows // 2
    blocks_b = reduce_line(sums[True], along_y)
    blocks_a = reduce_line(sums[False], along_x)
    up_b, down_b = messages(blocks_b)
    sp_b, sm_b = along_x(up_b, 1), along_x(down_b, -1)
    up_a, down_a = messages(blocks_a)
    sp_a, sm_a = along_y(up_a, 1), along_y(down_a, -1)
    sp_b, sm_b, _, _ = lax.optimization_barrier((sp_b, sm_b, up_a, down_a))
    own_b = (reduce_rest(blocks_b, sp_b, sm_b, along_x) + stream[half:].astype(F32)).astype(BF)
    own_a = (reduce_rest(blocks_a, sp_a, sm_a, along_y) + stream[:half].astype(F32)).astype(BF)
    stream_out = jnp.concatenate([own_a, own_b], axis=0)
    gain = norm_gain.reshape(GRID, cols)
    ones, twos = (0, 3), (1, 2)
    one_a, two_a, got_a = gather_line(own_a, along_y, along_x)
    one_b, two_b, got_b = gather_line(own_b, along_x, along_y)

    def pieces(a_blocks, b_blocks):
        out = [(v, [(far, d) for d in line], 0) for v, line, far in a_blocks]
        return out + [(v, [(d, far) for d in line], half) for v, line, far in b_blocks]

    near = pieces([(one_a, ones, 0), (two_a, twos, 0)], [(one_b, ones, 0), (two_b, twos, 0)])
    acc = qkv_part(rank, weights, gain, near, None, False)
    middle, last = [], []
    for got, second in ((got_a, along_x), (got_b, along_y)):
        end, _ = lax.optimization_barrier((got[3], acc))
        middle.append([(got[0], ones, 3), (got[1], ones, 1), (got[2], twos, 3), (got[3], twos, 1)])
        last.append([(second(got[0], 1), ones, 2), (second(end, -1), twos, 2)])
    acc = qkv_part(rank, weights, gain, pieces(*middle), acc, False)
    query, kv = qkv_part(rank, weights, gain, pieces(*last), acc, True)

    h = rows // 2
    place = context_rank.astype(jnp.int32).reshape(1)
    back = hop_z(kv, ((0, 1), (1, 2), (2, 3)))
    ahead = hop_z(kv, ((0, 3), (1, 0)))
    state = attend(place, query, [[kv], [swap_core(kv)]], (0, 0), None, False)
    back, ahead, state = lax.optimization_barrier((back, ahead, state))
    far_low = hop_z(back[:h], ((1, 2), (2, 3)))
    far_high = hop_z(ahead[h:], ((3, 2), (0, 3)))
    groups = [[back, swap_core(back)], [ahead, swap_core(ahead)]]
    state = attend(place, query, groups, (3, 1), state, False)
    far_low, far_high, state = lax.optimization_barrier((far_low, far_high, state))
    groups = [[far_low, far_high, swap_core(far_low), swap_core(far_high)]]
    context_out = attend(place, query, groups, (2,), state, True)
    return stream_out, context_out


def solution(mesh):
    placed = (
        P("context", None, "tensor"),
        P(None, None, "tensor"),
        P(None, "tensor"),
        P("context", "tensor"),
        P("tensor", None),
        P(),
        P(None, None, "tensor"),
    )
    return jax.shard_map(
        on_device,
        mesh=mesh,
        in_specs=placed,
        out_specs=(P("context", "tensor"), P("context", "tensor")),
        check_vma=False,
    )
```

```python
import math

import jax
import jax.numpy as jnp
from jax import lax
from jax.experimental import pallas as pl
from jax.experimental.pallas import tpu as pltpu
from jax.sharding import PartitionSpec as P

HD = 128
SIDE = 4
GRID = 16
HALO = 144
BF = jnp.bfloat16
F32 = jnp.float32


def params(mib):
    return pltpu.CompilerParams(vmem_limit_bytes=mib * 1024 * 1024)


def hop(value, dx, dy):
    pairs = []
    for x in range(SIDE):
        for y in range(SIDE):
            pairs.append((x * SIDE + y, ((x + dx) % SIDE) * SIDE + (y + dy) % SIDE))
    return lax.ppermute(value, "tensor", pairs)


def hop_z(value, steps):
    pairs = [(z * 2 + core, to * 2 + core) for z, to in steps for core in range(2)]
    return lax.ppermute(value, "context", pairs)


def swap_core(value):
    return lax.ppermute(value, "context", [(c, c ^ 1) for c in range(2 * SIDE)])


def toeplitz_body(taps, out):
    groups, width = taps.shape
    row = lax.broadcasted_iota(jnp.int32, (width, width), 0)
    col = lax.broadcasted_iota(jnp.int32, (width, width), 1)
    flip = (row + col == width - 1).astype(BF)
    reversed_taps = jnp.dot(taps[...], flip, preferred_element_type=F32)
    padded = jnp.concatenate([reversed_taps, jnp.zeros_like(reversed_taps)], axis=1)
    for g in range(groups):
        wide = jnp.broadcast_to(padded[g : g + 1, :], (width, 2 * width))
        out[g] = pltpu.roll(wide, 1, 1, stride=1, stride_axis=0).astype(BF)


def toeplitz(mr_filter):
    taps = mr_filter.T
    groups, width = taps.shape
    vmem = pl.BlockSpec(memory_space=pltpu.VMEM)
    return pl.pallas_call(
        toeplitz_body,
        in_specs=[vmem],
        out_specs=vmem,
        out_shape=jax.ShapeDtypeStruct((groups, width, 2 * width), BF),
        compiler_params=params(16),
        name="toeplitz",
    )(taps)


def fetch_body(source, out, sem):
    copy = pltpu.make_async_copy(source, out, sem)
    copy.start()
    copy.wait()


def fetch(source):
    return pl.pallas_call(
        fetch_body,
        in_specs=[pl.BlockSpec(memory_space=pl.ANY)],
        out_specs=pl.BlockSpec(memory_space=pltpu.VMEM),
        out_shape=jax.ShapeDtypeStruct(source.shape, source.dtype),
        scratch_shapes=[pltpu.SemaphoreType.DMA],
        compiler_params=params(16),
        name="fetch",
    )(pltpu.with_memory_space_constraint(source, pltpu.HBM))


def short(ref, taps, j, start, lanes):
    total = taps[j, 0:1, lanes] * ref[start : start + 128]
    for s in range(1, taps.shape[1]):
        total = total + taps[j, s : s + 1, lanes] * ref[start - s : start - s + 128]
    return total


def product_half(x1, x2, taps, kvs, block):
    lanes = slice(block * 128, (block + 1) * 128)
    for b in range(3):
        start = HALO - 128 + b * 128
        value = short(x1, taps, 1, start, lanes) * short(x2, taps, 2, start, lanes)
        kvs[b * 128 : (b + 1) * 128] = value.astype(BF)


def medium_half(toep, kvs, block):
    lhs = toep[block * 8 : (block + 1) * 8].reshape(8 * 128, 256)
    return [
        jnp.dot(lhs, kvs[b * 128 : b * 128 + 256], preferred_element_type=F32) for b in range(2)
    ]


def gated_half(x0, taps, fulls, block, gated):
    lanes = slice(block * 128, (block + 1) * 128)
    lane_group = lax.broadcasted_iota(jnp.int32, (128, 128), 1) // 16
    for b, full in enumerate(fulls):
        medium = full[0:128]
        for g in range(1, 8):
            medium = jnp.where(lane_group == g, full[g * 128 : (g + 1) * 128], medium)
        value = short(x0, taps, 0, 16 + b * 128, lanes) * medium
        gated[b * 128 : (b + 1) * 128, lanes] = value.astype(BF)


def piece_of(far, near):
    if far == 0:
        return "0", near
    if far == 2:
        return ("p", near) if near < 2 else ("m", near - 2)
    if far == 1:
        return ("1a", near) if near < 2 else ("p", near)
    return ("m", near + 2) if near < 2 else ("3b", near - 2)


def block_fetches(rank, names, swapped, w_hbm, wbuf, wsem):
    x, y = rank[0] // SIDE, rank[0] % SIDE
    cols = wbuf.shape[2]
    jobs = []
    for far in (2, 1, 3, 0):
        for near in range(SIDE):
            name, place = piece_of(far, near)
            if name not in names:
                continue
            dx, dy = (near, far) if swapped else (far, near)
            index = lax.rem(x + dx, SIDE) * SIDE + lax.rem(y + dy, SIDE)
            i = len(jobs)
            copy = pltpu.make_async_copy(
                w_hbm.at[:, pl.ds(pl.multiple_of(index * cols, cols), cols)],
                wbuf.at[i],
                wsem.at[i],
            )
            copy.start()
            jobs.append((copy, name, place))
    return jobs


def project_blocks(jobs, gated, wbuf, outs):
    for i, (copy, name, place) in enumerate(jobs):
        copy.wait()
        outs[name][place] = jnp.dot(gated[...], wbuf[i], preferred_element_type=F32).astype(BF)


def first_body(swapped, rank, feats, *refs):
    refs = list(refs)
    halo = None if swapped else refs.pop(0)
    taps, toep, w_hbm, gated, p, m, x0, x1, x2, kvs, wbuf, wsem = refs
    jobs = block_fetches(rank, ("p", "m"), swapped, w_hbm, wbuf, wsem)
    count = feats.shape[2] // 128
    for block in range(count):
        lanes = slice(block * 128, (block + 1) * 128)
        if swapped:
            x0[block] = feats[0, 240:512, lanes].astype(F32)
            x1[block] = feats[1, 112:512, lanes].astype(F32)
            x2[block] = feats[2, 112:512, lanes].astype(F32)
        else:
            x0[block, 0:16] = halo[0, HALO - 16 :, lanes].astype(F32)
            x0[block, 16:] = feats[0, 0:256, lanes].astype(F32)
            x1[block, 0:HALO] = halo[1, :, lanes].astype(F32)
            x1[block, HALO:] = feats[1, 0:256, lanes].astype(F32)
            x2[block, 0:HALO] = halo[2, :, lanes].astype(F32)
            x2[block, HALO:] = feats[2, 0:256, lanes].astype(F32)
    product_half(x1.at[0], x2.at[0], taps, kvs.at[0], 0)
    for block in range(count):
        fulls = medium_half(toep, kvs.at[block], block)
        if block + 1 < count:
            product_half(x1.at[block + 1], x2.at[block + 1], taps, kvs.at[block + 1], block + 1)
        gated_half(x0.at[block], taps, fulls, block, gated)
    project_blocks(jobs, gated, wbuf, {"p": p, "m": m})


def first(rank, feats, halo, taps, toep, w_out):
    half, cols = feats.shape[1] // 2, feats.shape[2]
    swapped = halo is None
    vmem = pl.BlockSpec(memory_space=pltpu.VMEM)
    smem = pl.BlockSpec(memory_space=pltpu.SMEM)
    hbm = pl.BlockSpec(memory_space=pl.ANY)
    args = [rank, feats] + ([] if swapped else [halo]) + [taps, toep, w_out]
    block = jax.ShapeDtypeStruct((4, half, cols), BF)

    def body(*refs):
        first_body(swapped, *refs)

    return pl.pallas_call(
        body,
        in_specs=[smem] + [vmem] * (len(args) - 2) + [hbm],
        out_specs=[vmem] * 3,
        out_shape=[jax.ShapeDtypeStruct((half, cols), BF), block, block],
        scratch_shapes=[
            pltpu.VMEM((cols // 128, half + 16, 128), F32),
            pltpu.VMEM((cols // 128, half + HALO, 128), F32),
            pltpu.VMEM((cols // 128, half + HALO, 128), F32),
            pltpu.VMEM((cols // 128, half + 128, 128), BF),
            pltpu.VMEM((8, cols, cols), BF),
            pltpu.SemaphoreType.DMA((8,)),
        ],
        compiler_params=params(20),
        cost_estimate=pl.CostEstimate(
            flops=4 * 10**9, transcendentals=0, bytes_accessed=w_out.size
        ),
        name="first",
    )(*args)


def rest_body(swapped, rank, gated, w_hbm, p1a, p3b, p0, wbuf, wsem):
    jobs = block_fetches(rank, ("1a", "3b", "0"), swapped, w_hbm, wbuf, wsem)
    project_blocks(jobs, gated, wbuf, {"1a": p1a, "3b": p3b, "0": p0})


def rest(rank, gated, w_out, swapped):
    half, cols = gated.shape
    vmem = pl.BlockSpec(memory_space=pltpu.VMEM)

    def body(*refs):
        rest_body(swapped, *refs)

    return pl.pallas_call(
        body,
        in_specs=[
            pl.BlockSpec(memory_space=pltpu.SMEM),
            vmem,
            pl.BlockSpec(memory_space=pl.ANY),
        ],
        out_specs=[vmem] * 3,
        out_shape=[jax.ShapeDtypeStruct((n, half, cols), BF) for n in (2, 2, 4)],
        scratch_shapes=[pltpu.VMEM((8, cols, cols), BF), pltpu.SemaphoreType.DMA((8,))],
        compiler_params=params(12),
        cost_estimate=pl.CostEstimate(
            flops=half * w_out.size, transcendentals=0, bytes_accessed=w_out.size
        ),
        name="rest",
    )(rank, gated, w_out)


def plus(*terms):
    total = terms[0].astype(F32)
    for term in terms[1:]:
        total = total + term.astype(F32)
    return total


def reduce_line(p, send):
    rp = send(p["p"], 1)
    rm = send(p["m"], -1)
    r1a = send(plus(p["1a"], rp[0:2]).astype(BF), 1)
    r3b = send(plus(p["3b"], rm[0:2]).astype(BF), -1)
    low = plus(p["0"][0:2], rm[2:4], r1a)
    high = plus(p["0"][2:4], rp[2:4], r3b)
    return low[0], low[1], high[0], high[1]


def messages(blocks):
    _, one, two, three = blocks
    h = one.shape[0] // 2
    up = jnp.concatenate([two[:h], one[h:]], axis=0).astype(BF)
    down = jnp.concatenate([two[h:], three[:h]], axis=0).astype(BF)
    return up, down


def reduce_rest(blocks, sp, sm, send):
    mine, one, _, three = blocks
    h = one.shape[0] // 2
    s1a = send(plus(one[:h], sp[:h]).astype(BF), 1)
    s3b = send(plus(three[h:], sm[:h]).astype(BF), -1)
    return plus(mine, jnp.concatenate([s1a, s3b], axis=0), jnp.concatenate([sm[h:], sp[h:]], axis=0))


def gather_line(own, first, second):
    h = own.shape[0] // 2
    back = first(own, 1)
    ahead = first(own, -1)
    far = jnp.concatenate([first(back[:h], 1), first(ahead[h:], -1)], axis=0)
    one = jnp.stack([own, back])
    two = jnp.stack([ahead, far])
    received = second(one, 1), second(one, -1), second(two, 1), second(two, -1)
    return one, two, received


def qkv_body(spec, has_acc, last, rank, w, gain, *refs):
    refs = list(refs)
    acc_in = refs.pop(0) if has_acc else None
    count = len(spec)
    pieces, refs = refs[:count], refs[count:]
    if last:
        q_out, kv_out, acc, xbuf = refs
    else:
        acc, xbuf = refs
    x, y = rank[0] // SIDE, rank[0] % SIDE
    part = w.shape[2]
    depth = gain.shape[1]
    filled = set()
    for (places, row), ref in zip(spec, pieces, strict=True):
        total = None
        rows = pl.ds(row, ref.shape[1])
        starts = []
        for k, place in enumerate(places):
            index = lax.rem(x + place[0], SIDE) * SIDE + lax.rem(y + place[1], SIDE)
            starts.append(pl.multiple_of(index * depth, depth))
            value = ref[k].astype(F32)
            for c in range(0, depth, 128):
                square = value[:, c : c + 128] * value[:, c : c + 128]
                total = square if total is None else total + square
            xbuf[k] = (value * gain[pl.ds(index, 1), :]).astype(BF)
        before = acc if row in filled else acc_in
        filled.add(row)
        for j in range(3):
            cols = slice(j * part, (j + 1) * part)
            term = None if before is None else before[rows, cols]
            for k, start in enumerate(starts):
                product = jnp.dot(
                    xbuf[k], w[j, pl.ds(start, depth), :], preferred_element_type=F32
                )
                term = product if term is None else term + product
            acc[rows, cols] = term
        acc[rows, 3 * part :] = total if before is None else before[rows, 3 * part :] + total
    if last:
        mean = jnp.sum(acc[:, 3 * part :], axis=1, keepdims=True) / (depth * GRID)
        scale = lax.rsqrt(mean + 1e-05)
        kv_out[...] = (acc[:, part : 3 * part] * scale).astype(BF)
        q_out[...] = (acc[:, :part] * scale).astype(BF)


def qkv_part(rank, w, gain, pieces, acc, last):
    spec = [(places, row) for _, places, row in pieces]
    part = w.shape[2]
    half, depth = pieces[0][0].shape[1:]
    rows = 2 * half
    vmem = pl.BlockSpec(memory_space=pltpu.VMEM)
    args = [rank, w, gain]
    specs = [pl.BlockSpec(memory_space=pltpu.SMEM), vmem, vmem]
    if acc is not None:
        args.append(acc)
        specs.append(vmem)
    for piece in pieces:
        args.append(piece[0])
        specs.append(vmem)
    scratch = [pltpu.VMEM((4, half, depth), BF)]
    acc_shape = (rows, 3 * part + 128)
    if last:
        out_shape = [
            jax.ShapeDtypeStruct((rows, part), BF),
            jax.ShapeDtypeStruct((rows, 2 * part), BF),
        ]
        out_specs = [vmem, vmem]
        scratch = [pltpu.VMEM(acc_shape, F32)] + scratch
    else:
        out_shape = jax.ShapeDtypeStruct(acc_shape, F32)
        out_specs = vmem

    def body(*refs):
        qkv_body(spec, acc is not None, last, *refs)

    blocks = sum(len(places) for places, _ in spec)
    return pl.pallas_call(
        body,
        in_specs=specs,
        out_specs=out_specs,
        out_shape=out_shape,
        scratch_shapes=scratch,
        compiler_params=params(24),
        cost_estimate=pl.CostEstimate(
            flops=blocks * 2 * half * depth * 3 * part,
            transcendentals=0,
            bytes_accessed=blocks * 6 * depth * part,
        ),
        name="qkv",
    )(*args)


TILE = 256


def attend_body(groups, shifts, own, last, rank, q, *refs):
    refs = list(refs)
    count = sum(groups)
    kvs, refs = refs[:count], refs[count:]
    if not own:
        m_in, l_in, acc_in = refs[:3]
        refs = refs[3:]
    if last:
        out, m_s, l_s, acc_s = refs
    else:
        m_s, l_s, acc_s = refs
    rows, part = q.shape
    heads = part // HD
    factor = HD ** (-0.5) * math.log2(math.e)
    if not own:
        m_s[...] = m_in[...]
        l_s[...] = l_in[...]
        acc_s[...] = acc_in[...]

    def score(pieces, h, r, first):
        query = q[r : r + TILE, h * HD : (h + 1) * HD]
        scores = []
        for ref in pieces:
            keys = r + TILE if first else ref.shape[0]
            s = lax.dot_general(
                query,
                ref[0:keys, h * HD : (h + 1) * HD],
                (((1,), (1,)), ((), ())),
                preferred_element_type=F32,
            )
            if first:
                qpos = r + lax.broadcasted_iota(jnp.int32, s.shape, 0)
                kpos = lax.broadcasted_iota(jnp.int32, s.shape, 1)
                s = jnp.where(kpos <= qpos, s, -1e30)
            scores.append(s)
        return scores

    def step(pieces, scores, h, r, first):
        top = None
        for s in scores:
            for c in range(0, s.shape[1], 128):
                piece = s[:, c : c + 128]
                top = piece if top is None else jnp.maximum(top, piece)
        top = jnp.max(top, axis=1, keepdims=True) * factor
        if first:
            new = top
        else:
            old = m_s[h, r : r + TILE]
            new = jnp.maximum(old, top)
        total, mixed = None, None
        for ref, s in zip(pieces, scores, strict=True):
            keys = s.shape[1]
            e = jnp.exp2(s * factor - new)
            for c in range(0, keys, 128):
                piece = e[:, c : c + 128]
                total = piece if total is None else total + piece
            value = ref[0:keys, part + h * HD : part + (h + 1) * HD]
            term = jnp.dot(e.astype(BF), value, preferred_element_type=F32)
            mixed = term if mixed is None else mixed + term
        if first:
            l_s[h, r : r + TILE] = total
            acc_s[h, r : r + TILE] = mixed
        else:
            fade = jnp.exp2(old - new)
            l_s[h, r : r + TILE] = l_s[h, r : r + TILE] * fade + total
            acc_s[h, r : r + TILE] = acc_s[h, r : r + TILE] * fade + mixed
        m_s[h, r : r + TILE] = new

    at = 0
    for i, n in enumerate(groups):
        pieces = kvs[at : at + n]
        at += n

        def whole(pieces=pieces, first=own and i == 0):
            tiles = [(h, r) for h in range(heads) for r in range(0, rows, TILE)]
            ready = [score(pieces, h, r, first) for h, r in tiles]
            for (h, r), scores in zip(tiles, ready, strict=True):
                step(pieces, scores, h, r, first)

        if own and i == 0:
            whole()
        else:
            z, core = rank[0] // 2, rank[0] % 2
            shift = shifts[i]
            pl.when(core == 1 if shift == 0 else lax.rem(z + shift, SIDE) < z)(whole)
    if last:
        for h in range(heads):
            total = jnp.sum(l_s[h], axis=1, keepdims=True)
            out[:, h * HD : (h + 1) * HD] = (acc_s[h] / total).astype(BF)


def attend(rank, q, groups, shifts, state, last):
    rows, width = q.shape
    heads = width // HD
    vmem = pl.BlockSpec(memory_space=pltpu.VMEM)
    state_shapes = [(heads, rows, 1), (heads, rows, 128), (heads, rows, HD)]
    pieces = [piece for group in groups for piece in group]
    counts = [len(group) for group in groups]
    args = [rank, q, *pieces] + (list(state) if state else [])
    if last:
        out_shape = jax.ShapeDtypeStruct((rows, width), BF)
        out_specs = vmem
        scratch = [pltpu.VMEM(shape, F32) for shape in state_shapes]
    else:
        out_shape = [jax.ShapeDtypeStruct(shape, F32) for shape in state_shapes]
        out_specs = [vmem] * 3
        scratch = []
    keys = sum(piece.shape[0] for piece in pieces)

    def body(*refs):
        attend_body(counts, shifts, state is None, last, *refs)

    return pl.pallas_call(
        body,
        in_specs=[pl.BlockSpec(memory_space=pltpu.SMEM)] + [vmem] * (len(args) - 1),
        out_specs=out_specs,
        out_shape=out_shape,
        scratch_shapes=scratch,
        compiler_params=params(24),
        cost_estimate=pl.CostEstimate(
            flops=4 * rows * keys * width,
            transcendentals=heads * rows * keys,
            bytes_accessed=4 * keys * width,
        ),
        name="attend",
    )(*args)


def on_device(features, se_filter, mr_filter, stream, w_out, norm_gain, w_qkv):
    rows, _, cols = features.shape
    feats = jnp.transpose(features, (1, 0, 2))
    taps = jnp.transpose(se_filter, (1, 0, 2))
    weights = jnp.transpose(w_qkv, (1, 0, 2))
    tensor_rank = lax.axis_index("tensor")
    context_rank = lax.axis_index("context")
    rank = tensor_rank.astype(jnp.int32).reshape(1)

    edge = feats[:, rows - HALO :]
    halo = lax.ppermute(edge, "context", [(c, c + 1) for c in range(2 * SIDE - 1)])
    toep = toeplitz(mr_filter)
    w_out = pltpu.with_memory_space_constraint(w_out, pltpu.HBM)
    blocks = {}
    for swapped in (True, False):
        gated, p, m = first(rank, feats, None if swapped else halo, taps, toep, w_out)
        blocks[swapped] = (gated, p, m)
    sums = {}
    for swapped in (True, False):
        gated, p, m = blocks[swapped]
        p1a, p3b, p0 = rest(rank, gated, w_out, swapped)
        sums[swapped] = {"p": p, "m": m, "1a": p1a, "3b": p3b, "0": p0}
    along_x = lambda v, d: hop(v, d, 0)
    along_y = lambda v, d: hop(v, 0, d)
    half = rows // 2
    blocks_b = reduce_line(sums[True], along_y)
    blocks_a = reduce_line(sums[False], along_x)
    up_b, down_b = messages(blocks_b)
    sp_b, sm_b = along_x(up_b, 1), along_x(down_b, -1)
    up_a, down_a = messages(blocks_a)
    sp_a, sm_a = along_y(up_a, 1), along_y(down_a, -1)
    sp_b, sm_b, _, _ = lax.optimization_barrier((sp_b, sm_b, up_a, down_a))
    own_b = (reduce_rest(blocks_b, sp_b, sm_b, along_x) + stream[half:].astype(F32)).astype(BF)
    own_a = (reduce_rest(blocks_a, sp_a, sm_a, along_y) + stream[:half].astype(F32)).astype(BF)
    stream_out = jnp.concatenate([own_a, own_b], axis=0)
    gain = norm_gain.reshape(GRID, cols)
    ones, twos = (0, 3), (1, 2)
    one_a, two_a, got_a = gather_line(own_a, along_y, along_x)
    one_b, two_b, got_b = gather_line(own_b, along_x, along_y)

    def pieces(a_blocks, b_blocks):
        out = [(v, [(far, d) for d in line], 0) for v, line, far in a_blocks]
        return out + [(v, [(d, far) for d in line], half) for v, line, far in b_blocks]

    near = pieces([(one_a, ones, 0), (two_a, twos, 0)], [(one_b, ones, 0), (two_b, twos, 0)])
    (one_a, one_b), _ = lax.optimization_barrier(((one_a, one_b), (got_a[0], got_b[0])))
    near = pieces([(one_a, ones, 0), (two_a, twos, 0)], [(one_b, ones, 0), (two_b, twos, 0)])
    acc = qkv_part(rank, weights, gain, near, None, False)
    middle, last = [], []
    for got, second in ((got_a, along_x), (got_b, along_y)):
        end, _ = lax.optimization_barrier((got[3], acc))
        middle.append([(got[0], ones, 3), (got[1], ones, 1), (got[2], twos, 3), (got[3], twos, 1)])
        last.append([(second(got[0], 1), ones, 2), (second(end, -1), twos, 2)])
    acc = qkv_part(rank, weights, gain, pieces(*middle), acc, False)
    query, kv = qkv_part(rank, weights, gain, pieces(*last), acc, True)

    h = rows // 2
    place = context_rank.astype(jnp.int32).reshape(1)
    back = hop_z(kv, ((0, 1), (1, 2), (2, 3)))
    ahead = hop_z(kv, ((0, 3), (1, 0)))
    state = attend(place, query, [[kv], [swap_core(kv)]], (0, 0), None, False)
    back, ahead, state = lax.optimization_barrier((back, ahead, state))
    far_low = hop_z(back[:h], ((1, 2), (2, 3)))
    far_high = hop_z(ahead[h:], ((3, 2), (0, 3)))
    groups = [[back, swap_core(back)], [ahead, swap_core(ahead)]]
    state = attend(place, query, groups, (3, 1), state, False)
    far_low, far_high, state = lax.optimization_barrier((far_low, far_high, state))
    groups = [[far_low, far_high, swap_core(far_low), swap_core(far_high)]]
    context_out = attend(place, query, groups, (2,), state, True)
    return stream_out, context_out


def solution(mesh):
    placed = (
        P("context", None, "tensor"),
        P(None, None, "tensor"),
        P(None, "tensor"),
        P("context", "tensor"),
        P("tensor", None),
        P(),
        P(None, None, "tensor"),
    )
    return jax.shard_map(
        on_device,
        mesh=mesh,
        in_specs=placed,
        out_specs=(P("context", "tensor"), P("context", "tensor")),
        check_vma=False,
    )
```
